128 devices in a mesh: gx: 8 (over y, z_lo), gz: 16 (over z_hi, x, core).
Axes of the slice: x: 4, y: 4, z: 4 (z_hi: 2, z_lo: 2; z = z_hi * 2 + z_lo), core: 2. Of those that a mesh axis runs over, the one named last changes fastest.
Arguments:
- velocity: float32 [3, 2048, 8, 4096], P(None, 'gx', None, 'gz'), may hold values from -6 to 6
- prior: float32 [3, 2048, 8, 4096], P(None, 'gx', None, 'gz'), may hold values from -3 to 3
Outputs:
- filtered: float32 [3, 2048, 8, 4096], P(None, 'gx', None, 'gz')
- advance: float32 [3, 2048, 8, 4096], P(None, 'gx', None, 'gz')
The draws below stay inside these ranges and needn't reach their ends.
All inputs are finite; a program needn't handle non-finite values.
Results may differ from the reference program's by a relative error of at most 0.0003.
Values sent between devices are 32-bit elements; how exact they have to be, the bound alone decides.
No kernel may reach another device: no remote copies, remote signals or barrier semaphores. Data moves between devices by JAX's collectives and lax.ppermute only.
A program may use at most 128 MiB of HBM per device.

```python
import math
import jax
import jax.numpy as jnp

PLANES = 8
NX = 2048
NZ = 4096


def wave_angles():
    waves_axial = max(1, NX // 64)
    waves_lateral = max(1, NZ // 64)
    axial_index = jnp.arange(NX, dtype=jnp.float32).reshape(NX, 1, 1)
    lateral_index = jnp.arange(NZ, dtype=jnp.float32).reshape(1, 1, NZ)
    angle_axial = 2.0 * math.pi * waves_axial / NX * axial_index
    angle_lateral = 2.0 * math.pi * waves_lateral / NZ * lateral_index
    return (angle_axial, angle_lateral)


def alternating(length, layout):
    signs = 1.0 - 2.0 * (jnp.arange(length, dtype=jnp.int32) % 2).astype(jnp.float32)
    return signs.reshape(layout)


def smooth_field(seed_key, mean_levels, ripple):
    subkeys = jax.random.split(seed_key, 2)
    phases = jax.random.uniform(subkeys[0], (3, 2), jnp.float32, -math.pi, math.pi)
    plane_gain = jax.random.uniform(subkeys[1], (3, 1, PLANES, 1), jnp.float32, 0.8, 1.2)
    angle_axial, angle_lateral = wave_angles()
    layers = []
    for component in range(3):
        ripple_wave = jnp.cos(angle_axial + phases[component, 0]) * jnp.cos(angle_lateral + phases[component, 1])
        layers.append(mean_levels[component] * plane_gain[component] + ripple * ripple_wave)
    return jnp.stack(layers)


def nyquist_field(seed_key, axial_levels, lateral_levels):
    phases = jax.random.uniform(seed_key, (3, 2), jnp.float32, -math.pi, math.pi)
    angle_axial, angle_lateral = wave_angles()
    sign_axial = alternating(NX, (NX, 1, 1))
    sign_lateral = alternating(NZ, (1, 1, NZ))
    layers = []
    for component in range(3):
        along_axial = axial_levels[component] * sign_axial * (1.0 + 0.15 * jnp.cos(angle_lateral + phases[component, 0]))
        along_lateral = lateral_levels[component] * sign_lateral * (1.0 + 0.15 * jnp.cos(angle_axial + phases[component, 1]))
        layers.append(jnp.broadcast_to(along_axial + along_lateral, (NX, PLANES, NZ)))
    return jnp.stack(layers)


def draw_velocity(key, part):
    subkeys = jax.random.split(key, 3)
    smooth_part = smooth_field(subkeys[0], (1.2, 0.3, 0.3), 0.4)
    nyquist_part = nyquist_field(subkeys[1], (2.4, 1.0, 0.0), (0.0, 1.0, 2.4))
    rough_part = 0.5 * jax.random.normal(subkeys[2], (3, NX, PLANES, NZ), jnp.float32)
    return jnp.clip(smooth_part + nyquist_part + rough_part, -6.0, 6.0)


def draw_prior(key, part):
    subkeys = jax.random.split(key, 2)
    smooth_part = smooth_field(subkeys[0], (0.6, 0.15, 0.15), 0.25)
    rough_part = 0.3 * jax.random.normal(subkeys[1], (3, NX, PLANES, NZ), jnp.float32)
    return jnp.clip(smooth_part + rough_part, -3.0, 3.0)


def setup_inputs(seed: int = 0) -> dict:
    arg_keys = jax.random.split(jax.random.key(seed), 3)
    velocity = draw_velocity(jax.random.fold_in(arg_keys[2], 71), 0)
    prior = draw_prior(jax.random.fold_in(arg_keys[2], 71), 0)
    return dict(velocity=velocity, prior=prior)


alpha_deriv = 1.0 / 3.0
alpha_filter = 0.49


def periodic_solve(rhs_values, alpha, axis):
    length = rhs_values.shape[axis]
    waves = jnp.arange(length // 2 + 1).astype(jnp.float32)
    symbol = 1.0 + 2.0 * alpha * jnp.cos(2.0 * math.pi * waves / length)
    layout = [1] * rhs_values.ndim
    layout[axis] = length // 2 + 1
    spectrum = jnp.fft.rfft(rhs_values, axis=axis) / symbol.reshape(layout)
    return jnp.fft.irfft(spectrum, n=length, axis=axis).astype(jnp.float32)


def derivative(field, axis, spacing):
    ahead_one = jnp.roll(field, -1, axis)
    behind_one = jnp.roll(field, 1, axis)
    ahead_two = jnp.roll(field, -2, axis)
    behind_two = jnp.roll(field, 2, axis)
    terms = (14.0 / 9.0) * (ahead_one - behind_one) / (2.0 * spacing) + (1.0 / 9.0) * (ahead_two - behind_two) / (4.0 * spacing)
    return periodic_solve(terms, alpha_deriv, axis)


def smooth(field, axis):
    alpha = alpha_filter
    weights = [(11.0 + 10.0 * alpha) / 16.0, (15.0 + 34.0 * alpha) / 32.0, (-3.0 + 6.0 * alpha) / 16.0, (1.0 - 2.0 * alpha) / 32.0]
    terms = weights[0] * field
    for offset in range(1, 4):
        terms = terms + 0.5 * weights[offset] * (jnp.roll(field, -offset, axis) + jnp.roll(field, offset, axis))
    return periodic_solve(terms, alpha, axis)


def reference(velocity, prior):
    spacing_x = 8.0 * math.pi / NX
    spacing_z = 3.0 * math.pi / NZ
    dt_step = 0.3 / (1.0 / spacing_x + 1.0 / spacing_z)
    axial = velocity[0]
    lateral = velocity[2]
    results = []
    advances = []
    for component in range(3):
        field = velocity[component]
        grad_x = derivative(field, 0, spacing_x)
        grad_z = derivative(field, 2, spacing_z)
        moved = -dt_step * (axial * grad_x + lateral * grad_z)
        provisional = field + (5.0 / 12.0) * moved - (17.0 / 60.0) * prior[component]
        results.append(smooth(smooth(provisional, 0), 2))
        advances.append(moved)
    return jnp.stack(results), jnp.stack(advances)
```

```python
import functools
import math

import jax
import jax.numpy as jnp
import numpy as np
from jax import lax
from jax.experimental import pallas as pl
from jax.experimental.pallas import tpu as pltpu
from jax.sharding import PartitionSpec as P

alpha_deriv = 1.0 / 3.0
alpha_filter = 0.49
rows_block = 32
near_deriv = 32
near_filter = 96
bf16 = jnp.bfloat16
f32 = jnp.float32
highest = lax.Precision.HIGHEST


def decay_rate(alpha):
    return (-1.0 + math.sqrt(1.0 - 4.0 * alpha * alpha)) / (2.0 * alpha)


def green_scale(alpha):
    return 1.0 / (1.0 + 2.0 * alpha * decay_rate(alpha))


def kernel_values(offsets, taps, alpha):
    offsets = np.asarray(offsets, dtype=np.float64)
    total = np.zeros_like(offsets)
    for shift, weight in taps.items():
        total = total + weight * green_scale(alpha) * np.power(
            decay_rate(alpha), np.abs(offsets - shift)
        )
    return total


def deriv_taps(spacing):
    near = 14.0 / 9.0 / (2.0 * spacing)
    far = 1.0 / 9.0 / (4.0 * spacing)
    return {1: near, -1: -near, 2: far, -2: -far}


def filter_taps():
    taps = {0: (11.0 + 10.0 * alpha_filter) / 16.0}
    weights = (
        (15.0 + 34.0 * alpha_filter) / 32.0,
        (-3.0 + 6.0 * alpha_filter) / 16.0,
        (1.0 - 2.0 * alpha_filter) / 32.0,
    )
    for shift, weight in enumerate(weights, 1):
        taps[shift] = 0.5 * weight
        taps[-shift] = 0.5 * weight
    return taps


def parts(values):
    high = values.astype(bf16)
    low = (values - high.astype(f32)).astype(bf16)
    return high, low


def np_parts(values):
    values = np.asarray(values, dtype=np.float32)
    high = values.astype(bf16)
    low = (values - high.astype(np.float32)).astype(bf16)
    return high, low


def band_matrix(count, taps, alpha, factor):
    source = np.arange(count)[:, None]
    target = np.arange(count)[None, :]
    high, low = np_parts(factor * kernel_values(source - target, taps, alpha))
    return np.concatenate([high, high, low], axis=0)


def edge_functionals(count, taps, alpha, factor, terms, group):
    source = np.arange(count)
    table = np.zeros((2 * group, 3 * count))
    for term in range(terms):
        right = factor * kernel_values(source - (count + term), taps, alpha)
        left = factor * kernel_values(source + 1 + term, taps, alpha)
        for comp in range(3):
            span = slice(comp * count, (comp + 1) * count)
            table[term * 3 + comp, span] = right
            table[group + term * 3 + comp, span] = left
    return table


def edge_profiles(count, alpha, terms, group):
    cell = np.arange(count)
    table = np.zeros((3, 2 * group, count))
    rate = decay_rate(alpha)
    for term in range(terms):
        if term < terms - 1:
            shape = (cell == term) * 1.0
        else:
            shape = np.where(cell >= term, np.power(rate, np.maximum(cell - term, 0)), 0.0)
        for comp in range(3):
            table[comp, term * 3 + comp] = shape
            table[comp, group + term * 3 + comp] = shape[::-1]
    return table


def padded_profiles(table):
    high, low = np_parts(table)
    stacked = np.concatenate([high, high, low], axis=1)
    rest = np.zeros((3, 128 - stacked.shape[1], stacked.shape[2]), dtype=bf16)
    return np.concatenate([stacked, rest], axis=1)


def spread_columns(left, right):
    both = jnp.concatenate([left, right], axis=0)
    high = both.astype(bf16).astype(f32)
    low = both - high
    rest = jnp.zeros((128 - 3 * both.shape[0], both.shape[1]), f32)
    return jnp.concatenate([high, low, high, rest], axis=0).T.astype(bf16)


def contract_last(a, b):
    return lax.dot_general(a, b, (((1,), (1,)), ((), ())), preferred_element_type=f32)


def dot(a, b):
    return jnp.dot(a, b, preferred_element_type=f32)


def edge_values(functional, highs, lows, count):
    half = functional.shape[0] // 2
    first = None
    second = None
    for comp in range(3):
        span = slice(comp * count, (comp + 1) * count)
        a = contract_last(functional[:, span], highs[comp])
        b = contract_last(functional[:half, span], lows[comp])
        first = a if first is None else first + a
        second = b if second is None else second + b
    return first[:half] + first[half:] + second


def x_edge_body(rate, low_ref, high_ref, right_ref, left_ref):
    last = near_deriv - 1
    total = high_ref[:, 0]
    for i in range(1, last):
        total = rate * total + high_ref[:, i]
    right_ref[0] = total
    right_ref[1] = high_ref[:, last]
    total = low_ref[:, last]
    for i in range(last - 1, 0, -1):
        total = rate * total + low_ref[:, i]
    left_ref[0] = total
    left_ref[1] = low_ref[:, 0]


def z_edge_body(v_ref, functional_ref, right_ref, left_ref):
    rows = v_ref.shape[1] * v_ref.shape[2]
    count = v_ref.shape[3]
    highs, lows = [], []
    for comp in range(3):
        high, low = parts(v_ref[comp].reshape(rows, count))
        highs.append(high)
        lows.append(low)
    out = edge_values(functional_ref[...], highs, lows, count)
    group = right_ref.shape[0]
    right_ref[...] = out[:group]
    left_ref[...] = out[group:]


def advance_body(
    n_blocks, consts,
    v_ref, prior_ref, xl_ref, xr_ref, zl_ref, zr_ref, dz_ref, pz_ref, fz_ref, wz_ref,
    adv_ref, q_ref, zright_ref, zleft_ref, xright_ref, xleft_ref,
    back, tail, lead, prov, qlead, qback, power,
):
    step = pl.program_id(0)
    size = v_ref.shape[1]
    count = v_ref.shape[3]
    rows = size * v_ref.shape[2]
    rate = consts["rate_d"]
    ratio = consts["ratio_d"]

    @pl.when(step == 0)
    def _():
        tail[0] = xr_ref[0]
        tail[1] = xr_ref[1]

    @pl.when(step < n_blocks)
    def _():
        base = (n_blocks - 1 - step) * size
        total = tail[0]
        nxt = tail[1]
        for i in range(size - 1, -1, -1):
            back[base + i] = total + ratio * nxt
            total = rate * total + nxt
            nxt = v_ref[:, i]
        tail[0] = total
        tail[1] = nxt

    @pl.when(step == n_blocks)
    def _():
        lead[0] = xl_ref[0]
        lead[1] = xl_ref[1]
        qlead[...] = jnp.zeros_like(qlead)
        qback[...] = jnp.zeros_like(qback)
        power[0] = 1.0

    @pl.when(step >= n_blocks)
    def _():
        base = (step - n_blocks) * size
        columns = spread_columns(zl_ref[...], zr_ref[...])
        slopes = []
        for comp in range(3):
            high, low = parts(v_ref[comp].reshape(rows, count))
            lhs = jnp.concatenate([high, low, high], axis=1)
            slope = dot(lhs, dz_ref[...]) + dot(columns, pz_ref[comp])
            slopes.append(slope.reshape(size, rows // size, count))
        total = lead[0]
        prev = lead[1]
        for i in range(size):
            here = v_ref[:, i]
            gx = back[base + i] - (total + ratio * prev)
            total = rate * total + prev
            prev = here
            ux = consts["x_factor"] * here[0]
            dz = jnp.stack([slopes[comp][i] for comp in range(3)])
            adv = ux[None] * gx + here[2][None] * dz
            adv_ref[:, i] = adv
            prov[:, i] = here + (5.0 / 12.0) * adv - (17.0 / 60.0) * prior_ref[:, i]
        lead[0] = total
        lead[1] = prev
        highs, lows = [], []
        for comp in range(3):
            high, low = parts(prov[comp].reshape(rows, count))
            highs.append(high)
            lows.append(low)
            lhs = jnp.concatenate([high, low, high], axis=1)
            q_ref[comp] = dot(lhs, fz_ref[...]).reshape(size, rows // size, count)
        out = edge_values(wz_ref[...], highs, lows, count)
        group = zright_ref.shape[0]
        zright_ref[...] = out[:group]
        zleft_ref[...] = out[group:]
        rate_f = consts["rate_f"]
        total = qlead[0]
        one = qlead[1]
        two = qlead[2]
        for i in range(size):
            total = rate_f * total + two
            two = one
            one = q_ref[:, i]
        qlead[0] = total
        qlead[1] = one
        qlead[2] = two
        total = q_ref[:, size - 1]
        for i in range(size - 2, 1, -1):
            total = rate_f * total + q_ref[:, i]

        @pl.when(step == n_blocks)
        def _():
            qback[...] = total
            xleft_ref[1] = q_ref[:, 0]
            xleft_ref[2] = q_ref[:, 1]
            power[0] = consts["power_f"] / (rate_f * rate_f)

        @pl.when(step > n_blocks)
        def _():
            full = rate_f * (rate_f * total + q_ref[:, 1]) + q_ref[:, 0]
            qback[...] = qback[...] + power[0] * full
            power[0] = power[0] * consts["power_f"]

        @pl.when(step == 2 * n_blocks - 1)
        def _():
            xleft_ref[0] = qback[...]
            xright_ref[0] = qlead[0]
            xright_ref[1] = qlead[1]
            xright_ref[2] = qlead[2]


def corner_body(xright_ref, xleft_ref, zl_ref, zr_ref, tr_ref, tl_ref, pc_ref, right_ref, left_ref):
    near = tr_ref.shape[0]
    planes = jnp.concatenate([zl_ref[...], zr_ref[...]], axis=0)
    span = planes.shape[1]
    hi = jnp.dot(planes[:, span - near:], tr_ref[...], precision=highest, preferred_element_type=f32)
    lo = jnp.dot(planes[:, :near], tl_ref[...], precision=highest, preferred_element_type=f32)
    terms = right_ref.shape[0]
    lines = right_ref.shape[2]
    for comp in range(3):
        for res, src_ref, dst_ref in ((hi, xright_ref, right_ref), (lo, xleft_ref, left_ref)):
            add = lax.dot_general(
                res, pc_ref[comp], (((0,), (0,)), ((), ())),
                precision=highest, preferred_element_type=f32,
            )
            for term in range(terms):
                dst_ref[term, comp] = src_ref[term, comp] + add[term * lines:(term + 1) * lines]


def filter_body(
    n_blocks, consts,
    q_ref, xl_ref, xr_ref, zl_ref, zr_ref, pz_ref,
    out_ref,
    full, back, tail, lead,
):
    step = pl.program_id(0)
    size = q_ref.shape[1]
    count = q_ref.shape[3]
    lines = q_ref.shape[2]
    rate = consts["rate_f"]

    @pl.when(step == 0)
    def _():
        for k in range(3):
            tail[k] = xr_ref[k]
        full[n_blocks * size] = xr_ref[1]
        full[n_blocks * size + 1] = xr_ref[2]

    @pl.when(step < n_blocks)
    def _():
        base = (n_blocks - 1 - step) * size
        columns = spread_columns(zl_ref[...], zr_ref[...])
        adds = [dot(columns, pz_ref[comp]).reshape(size, lines, count) for comp in range(3)]
        total, one, two = tail[0], tail[1], tail[2]
        for i in range(size - 1, -1, -1):
            back[base + i] = total
            here = q_ref[:, i] + jnp.stack([adds[comp][i] for comp in range(3)])
            full[base + i] = here
            total = rate * total + two
            two = one
            one = here
        tail[0] = total
        tail[1] = one
        tail[2] = two

    @pl.when(step == n_blocks)
    def _():
        for k in range(3):
            lead[k] = xl_ref[k]

    @pl.when(step >= n_blocks)
    def _():
        base = (step - n_blocks) * size
        total, one, two = lead[0], lead[1], lead[2]
        here = full[base]
        ahead = full[base + 1]
        for i in range(size):
            further = full[base + i + 2]
            value = (
                consts["k3"] * (total + back[base + i])
                + consts["k0"] * here
                + consts["k1"] * (ahead + one)
                + consts["k2"] * (further + two)
            )
            out_ref[:, i] = value
            total = rate * total + two
            two = one
            one = here
            here = ahead
            ahead = further
        lead[0] = total
        lead[1] = one
        lead[2] = two


def whole(shape):
    return pl.BlockSpec(shape, lambda t: (0,) * len(shape))


def ring(count, step):
    return [(i, (i + step) % count) for i in range(count)]


def swap(right, left, axis):
    count = lax.axis_size(axis)
    return (
        lax.ppermute(right, axis, ring(count, 1)),
        lax.ppermute(left, axis, ring(count, -1)),
    )


def shards(velocity, prior):
    comps, cells_x, lines, cells_z = velocity.shape
    spacing_x = 8.0 * math.pi / (cells_x * lax.axis_size("gx"))
    spacing_z = 3.0 * math.pi / (cells_z * lax.axis_size("gz"))
    dt_step = 0.3 / (1.0 / spacing_x + 1.0 / spacing_z)
    rate_d = decay_rate(alpha_deriv)
    rate_f = decay_rate(alpha_filter)
    size = rows_block
    n_blocks = cells_x // size
    rows = size * lines
    span = cells_x * lines

    kd = kernel_values([1, 2], deriv_taps(spacing_x), alpha_deriv)
    kf = kernel_values([0, 1, 2, 3], filter_taps(), alpha_filter)
    consts = {
        "rate_d": rate_d,
        "ratio_d": float(kd[0] / kd[1]),
        "x_factor": float(-dt_step * kd[1]),
        "rate_f": rate_f,
        "power_f": float(rate_f ** size),
        "k0": float(kf[0]),
        "k1": float(kf[1]),
        "k2": float(kf[2]),
        "k3": float(kf[3]),
    }

    plane = (comps, lines, cells_z)
    big = lambda idx: pl.BlockSpec((comps, size, lines, cells_z), lambda t: (0, idx(t), 0, 0))
    edge = (2,) + plane
    xr_send, xl_send = pl.pallas_call(
        functools.partial(x_edge_body, rate_d),
        grid=(1,),
        in_specs=[
            pl.BlockSpec((comps, near_deriv, lines, cells_z), lambda t: (0, 0, 0, 0)),
            pl.BlockSpec(
                (comps, near_deriv, lines, cells_z), lambda t: (0, cells_x // near_deriv - 1, 0, 0)
            ),
        ],
        out_specs=[whole(edge)] * 2,
        out_shape=[jax.ShapeDtypeStruct(edge, f32)] * 2,
        name="x_edge",
    )(velocity, velocity)
    xl, xr = swap(xr_send, xl_send, "gx")

    group_d = 8
    taps_z = deriv_taps(spacing_z)
    wd = edge_functionals(cells_z, taps_z, alpha_deriv, -dt_step, 2, group_d)
    wd = jnp.asarray(np.concatenate(np_parts(wd), axis=0))
    zr_send, zl_send = pl.pallas_call(
        z_edge_body,
        grid=(n_blocks,),
        in_specs=[big(lambda t: t), whole(wd.shape)],
        out_specs=[pl.BlockSpec((group_d, rows), lambda t: (0, t))] * 2,
        out_shape=[jax.ShapeDtypeStruct((group_d, span), f32)] * 2,
        name="z_edge",
    )(velocity, wd)
    zl, zr = swap(zr_send, zl_send, "gz")

    group_f = 16
    dz = jnp.asarray(band_matrix(cells_z, taps_z, alpha_deriv, -dt_step))
    pd = jnp.asarray(padded_profiles(edge_profiles(cells_z, alpha_deriv, 2, group_d)))
    fz = jnp.asarray(band_matrix(cells_z, filter_taps(), alpha_filter, 1.0))
    wf = edge_functionals(cells_z, filter_taps(), alpha_filter, 1.0, 3, group_f)
    wf = jnp.asarray(np.concatenate(np_parts(wf), axis=0))
    profiles_f = edge_profiles(cells_z, alpha_filter, 3, group_f)
    pf = jnp.asarray(padded_profiles(profiles_f))
    later = lambda t: jnp.maximum(t - n_blocks, 0)
    turn = lambda t: jnp.where(t < n_blocks, n_blocks - 1 - t, t - n_blocks)
    edge3 = (3,) + plane
    advance, q, zr_send, zl_send, xr_part, xl_part = pl.pallas_call(
        functools.partial(advance_body, n_blocks, consts),
        grid=(2 * n_blocks,),
        in_specs=[
            big(turn), big(later), whole(edge), whole(edge),
            pl.BlockSpec((group_d, rows), lambda t: (0, later(t))),
            pl.BlockSpec((group_d, rows), lambda t: (0, later(t))),
            whole(dz.shape), whole(pd.shape), whole(fz.shape), whole(wf.shape),
        ],
        out_specs=[
            big(later), big(later),
            pl.BlockSpec((group_f, rows), lambda t: (0, later(t))),
            pl.BlockSpec((group_f, rows), lambda t: (0, later(t))),
            whole(edge3), whole(edge3),
        ],
        out_shape=[
            jax.ShapeDtypeStruct(velocity.shape, f32),
            jax.ShapeDtypeStruct(velocity.shape, f32),
            jax.ShapeDtypeStruct((group_f, span), f32),
            jax.ShapeDtypeStruct((group_f, span), f32),
            jax.ShapeDtypeStruct(edge3, f32),
            jax.ShapeDtypeStruct(edge3, f32),
        ],
        scratch_shapes=[
            pltpu.VMEM((cells_x,) + plane, f32),
            pltpu.VMEM((2,) + plane, f32),
            pltpu.VMEM((2,) + plane, f32),
            pltpu.VMEM((comps, size, lines, cells_z), f32),
            pltpu.VMEM((3,) + plane, f32),
            pltpu.VMEM(plane, f32),
            pltpu.SMEM((1,), f32),
        ],
        name="advance",
    )(velocity, prior, xl, xr, zl, zr, dz, pd, fz, wf)
    zl, zr = swap(zr_send, zl_send, "gz")

    near = near_filter * lines
    cell = np.arange(cells_x)[:, None, None, None]
    line = (np.arange(lines)[None, :, None, None] == np.arange(lines)[None, None, None, :]) * 1.0
    back_off = cells_x - 3 - cell
    grow = np.where(back_off >= 0, np.power(rate_f, np.maximum(back_off, 0)), 0.0)
    pick = np.concatenate([grow, cell == cells_x - 1, cell == cells_x - 2], axis=2) * 1.0
    right_table = (pick * line).reshape(span, 3 * lines)
    left_table = (pick[::-1] * line).reshape(span, 3 * lines)
    widen = lambda t: np.concatenate([t, np.zeros((near, 128 - t.shape[1]))], axis=1)
    tr = jnp.asarray(widen(right_table[span - near:]), f32)
    tl = jnp.asarray(widen(left_table[:near]), f32)
    pc = jnp.asarray(profiles_f, f32)
    xr_send, xl_send = pl.pallas_call(
        corner_body,
        grid=(1,),
        in_specs=[
            whole(edge3), whole(edge3), whole((group_f, span)), whole((group_f, span)),
            whole(tr.shape), whole(tl.shape), whole(pc.shape),
        ],
        out_specs=[whole(edge3)] * 2,
        out_shape=[jax.ShapeDtypeStruct(edge3, f32)] * 2,
        name="corner",
    )(xr_part, xl_part, zl, zr, tr, tl, pc)
    xl, xr = swap(xr_send, xl_send, "gx")

    early = lambda t: jnp.maximum(n_blocks - 1 - t, 0)
    filtered = pl.pallas_call(
        functools.partial(filter_body, n_blocks, consts),
        grid=(2 * n_blocks,),
        in_specs=[
            big(early), whole(edge3), whole(edge3),
            pl.BlockSpec((group_f, rows), lambda t: (0, early(t))),
            pl.BlockSpec((group_f, rows), lambda t: (0, early(t))),
            whole(pf.shape),
        ],
        out_specs=big(later),
        out_shape=jax.ShapeDtypeStruct(velocity.shape, f32),
        scratch_shapes=[
            pltpu.VMEM((cells_x + 2,) + plane, f32),
            pltpu.VMEM((cells_x,) + plane, f32),
            pltpu.VMEM((3,) + plane, f32),
            pltpu.VMEM((3,) + plane, f32),
        ],
        name="filter",
    )(q, xl, xr, zl, zr, pf)
    return (filtered, advance)


def solution(mesh):
    placed = P(None, "gx", None, "gz")
    return jax.shard_map(
        shards,
        mesh=mesh,
        in_specs=(placed, placed),
        out_specs=(placed, placed),
        check_vma=False,
    )
```

```python
import functools
import math

import jax
import jax.numpy as jnp
import numpy as np
from jax import lax
from jax.experimental import pallas as pl
from jax.experimental.pallas import tpu as pltpu
from jax.sharding import PartitionSpec as P

alpha_deriv = 1.0 / 3.0
alpha_filter = 0.49
rows_edge = 64
rows_block = 64
rows_sub = 16
rows_filter = 64
near_deriv = 32
near_filter = 96
LANES = 128
bf16 = jnp.bfloat16
f32 = jnp.float32


def decay_rate(alpha):
    return (-1.0 + math.sqrt(1.0 - 4.0 * alpha * alpha)) / (2.0 * alpha)


def green_scale(alpha):
    return 1.0 / (1.0 + 2.0 * alpha * decay_rate(alpha))


def kernel_values(offsets, taps, alpha):
    offsets = np.asarray(offsets, dtype=np.float64)
    total = np.zeros_like(offsets)
    for shift, weight in taps.items():
        total = total + weight * green_scale(alpha) * np.power(
            decay_rate(alpha), np.abs(offsets - shift)
        )
    return total


def deriv_taps(spacing):
    near = 14.0 / 9.0 / (2.0 * spacing)
    far = 1.0 / 9.0 / (4.0 * spacing)
    return {1: near, -1: -near, 2: far, -2: -far}


def filter_taps():
    taps = {0: (11.0 + 10.0 * alpha_filter) / 16.0}
    weights = (
        (15.0 + 34.0 * alpha_filter) / 32.0,
        (-3.0 + 6.0 * alpha_filter) / 16.0,
        (1.0 - 2.0 * alpha_filter) / 32.0,
    )
    for shift, weight in enumerate(weights, 1):
        taps[shift] = 0.5 * weight
        taps[-shift] = 0.5 * weight
    return taps


def parts(values):
    high = values.astype(bf16)
    low = (values - high.astype(f32)).astype(bf16)
    return high, low


def np_parts(values):
    values = np.asarray(values, dtype=np.float32)
    high = values.astype(bf16)
    low = (values - high.astype(np.float32)).astype(bf16)
    return high, low


def band_matrix(count, taps, alpha, factor):
    source = np.arange(count)[:, None]
    target = np.arange(count)[None, :]
    high, low = np_parts(factor * kernel_values(source - target, taps, alpha))
    return np.concatenate([high, high, low], axis=0)


def edge_profiles(count, alpha, terms, group):
    cell = np.arange(count)
    table = np.zeros((2 * group, count))
    rate = decay_rate(alpha)
    for term in range(terms):
        if term < terms - 1:
            shape = (cell == term) * 1.0
        else:
            shape = np.where(cell >= term, np.power(rate, np.maximum(cell - term, 0)), 0.0)
        for comp in range(3):
            table[term * 3 + comp] = shape
            table[group + term * 3 + comp] = shape[::-1]
    return table


def padded_profiles(table):
    high, low = np_parts(table)
    rest = np.zeros((LANES - 3 * table.shape[0], table.shape[1]), dtype=bf16)
    return np.concatenate([high, high, low, rest], axis=0)


def component_masks(terms, group):
    lane = np.arange(LANES)
    row = lane % group
    masks = [(lane < 6 * group) & (row < 3 * terms) & (row % 3 == comp) for comp in range(3)]
    return jnp.asarray(np.stack(masks)[:, None, :], bf16)


def spread_columns(left, right):
    both = jnp.concatenate([left, right], axis=0)
    high = both.astype(bf16).astype(f32)
    low = both - high
    rest = jnp.zeros((128 - 3 * both.shape[0], both.shape[1]), f32)
    return jnp.concatenate([high, low, high, rest], axis=0).T.astype(bf16)


def dot(a, b):
    return jnp.dot(a, b, preferred_element_type=f32)


def edge_body(rate, v_ref, weight_ref, zright_ref, zleft_ref, xright_ref, xleft_ref):
    step = pl.program_id(0)
    size, lines, count = v_ref.shape[1:]
    near = weight_ref.shape[1]
    group = LANES // lines
    left_lane = lax.broadcasted_iota(jnp.int32, (LANES, LANES), 1) < LANES // 2
    for comp in range(3):
        for part in range(size // group):
            block = v_ref[comp, part * group:(part + 1) * group].reshape(LANES, count)
            both = jnp.where(left_lane, block[:, :LANES], block[:, count - LANES:]).T
            span = slice(part * LANES, (part + 1) * LANES)
            for term in range(2):
                row = term * 3 + comp
                zright_ref[row:row + 1, span] = jnp.sum(
                    both[LANES - near:] * weight_ref[term], axis=0, keepdims=True
                )
                zleft_ref[row:row + 1, span] = jnp.sum(
                    both[:near] * weight_ref[2 + term], axis=0, keepdims=True
                )
    for row in range(6, 8):
        zright_ref[row:row + 1, :] = jnp.zeros((1, size * lines), f32)
        zleft_ref[row:row + 1, :] = jnp.zeros((1, size * lines), f32)

    @pl.when(step == 0)
    def _():
        total = v_ref[:, near_deriv - 1]
        for i in range(near_deriv - 2, -1, -1):
            total = rate * total + v_ref[:, i]
        xleft_ref[0] = total
        xleft_ref[1] = v_ref[:, 0]

    @pl.when(step == pl.num_programs(0) - 1)
    def _():
        total = v_ref[:, size - near_deriv]
        for i in range(size - near_deriv + 1, size):
            total = rate * total + v_ref[:, i]
        xright_ref[0] = total
        xright_ref[1] = v_ref[:, size - 1]


def weighted_rows(ref, weights):
    sums = [None] * 4
    for k, (row, weight) in enumerate(weights):
        term = weight * ref[:, row]
        sums[k % 4] = term if sums[k % 4] is None else sums[k % 4] + term
    return (sums[0] + sums[1]) + (sums[2] + sums[3])


def advance_body(
    n_blocks, consts,
    v_ref, prior_ref, xl_ref, xr_ref, zl_ref, zr_ref, dz_ref, mask_ref, fz_ref,
    adv_ref, q_ref, zright_ref, zleft_ref, xright_ref, xleft_ref,
    back, base, slope, firsts, high, low, ends, tail, lead, qsum,
):
    step = pl.program_id(0)
    size, lines, count = v_ref.shape[1:]
    sub = rows_sub
    rate = consts["rate_d"]
    ratio = consts["ratio_d"]

    @pl.when(step == 0)
    def _():
        tail[...] = xr_ref[0]
        back[n_blocks * size] = xr_ref[0]
        firsts[n_blocks] = xr_ref[1]

    @pl.when(step < n_blocks)
    def _():
        chunk = n_blocks - 1 - step
        start = chunk * size
        columns = spread_columns(zl_ref[...], zr_ref[...])
        masked = [columns * mask_ref[comp] for comp in range(3)]
        total = tail[...]
        for part in range(size // sub - 1, -1, -1):
            rows = slice(part * sub, (part + 1) * sub)
            flat = slice(part * sub * lines, (part + 1) * sub * lines)
            hi, lo = parts(v_ref[:, rows].reshape(3 * sub * lines, count))
            edge = jnp.concatenate([masked[comp][flat] for comp in range(3)], axis=0)
            lhs = jnp.concatenate([hi, lo, hi, edge], axis=1)
            slope[chunk, :, rows] = dot(lhs, dz_ref[...]).reshape(3, sub, lines, count)
            for i in range((part + 1) * sub - 1, part * sub - 1, -1):
                here = v_ref[:, i]
                total = here + rate * total
                back[start + i] = total
                base[start + i] = 2.4 * here - 0.68 * prior_ref[:, i]
        tail[...] = total
        firsts[chunk] = v_ref[:, 0]

    @pl.when(step == n_blocks)
    def _():
        before = (xl_ref[0] + rate * back[0]) * (1.0 / (1.0 - rate * rate))
        value = back[0] + rate * before
        lead[0] = value
        lead[1] = before + ratio * xl_ref[1]
        lead[2] = value + ratio * v_ref[:, 0]
        qsum[...] = jnp.zeros_like(qsum)

    @pl.when(step >= n_blocks)
    def _():
        chunk = step - n_blocks
        start = chunk * size
        value, behind, level = lead[0], lead[1], lead[2]
        left_lane = lax.broadcasted_iota(jnp.int32, (3, 2 * lines, LANES), 2) < LANES // 2
        left_tile = lax.broadcasted_iota(jnp.int32, (LANES, LANES), 1) < LANES // 2
        here = v_ref[:, 0]
        for part in range(size // sub):
            for i in range(part * sub, (part + 1) * sub, 2):
                pair = []
                for j in (i, i + 1):
                    ahead = v_ref[:, j + 1] if j + 1 < size else firsts[chunk + 1]
                    value = back[start + j + 1] + rate * value
                    above = value + ratio * ahead
                    gx = above - behind
                    behind = level
                    level = above
                    ux = consts["x_factor"] * here[0]
                    adv = ux[None] * gx + here[2][None] * slope[chunk, :, j]
                    adv_ref[:, j] = adv
                    pair.append(base[start + j] + adv)
                    here = ahead
                both = jnp.concatenate(pair, axis=1)
                flat = slice(i * lines, (i + 2) * lines)
                ends[:, flat] = jnp.where(left_lane, both[:, :, :LANES], both[:, :, count - LANES:])
                hi, lo = parts(both)
                high[:, flat] = hi
                low[:, flat] = lo
            rows = slice(part * sub * lines, (part + 1) * sub * lines)
            hi = high[:, rows].reshape(3 * sub * lines, count)
            lo = low[:, rows].reshape(3 * sub * lines, count)
            lhs = jnp.concatenate([hi, lo, hi], axis=1)
            q = dot(lhs, fz_ref[...])
            q_ref[:, part * sub:(part + 1) * sub] = q.reshape(3, sub, lines, count)
            for comp in range(3):
                for piece in range(sub * lines // LANES):
                    at = comp * sub * lines + piece * LANES
                    qe = q[at:at + LANES]
                    qt = jnp.where(left_tile, qe[:, :LANES], qe[:, count - LANES:]).T
                    first = part * sub * lines + piece * LANES
                    lanes = slice(first, first + LANES)
                    ft = ends[comp, lanes].T
                    for ref, order in ((zright_ref, (127, 126, 125)), (zleft_ref, (0, 1, 2))):
                        f0, f1, f2 = [ft[k:k + 1] for k in order]
                        qq = qt[order[0]:order[0] + 1]
                        r = consts["rate_f"]
                        cs = qq - consts["e0"] * f0 - consts["e1"] * f1 - consts["e2"] * f2
                        ref[comp:comp + 1, lanes] = r * cs + consts["e1"] * f0 + consts["e2"] * f1
                        ref[3 + comp:4 + comp, lanes] = (r * r) * cs + consts["e2"] * f0
                        ref[6 + comp:7 + comp, lanes] = (r * r * r) * cs
        lead[0] = value
        lead[1] = behind
        lead[2] = level
        for ref in (zright_ref, zleft_ref):
            ref[9:16, :] = jnp.zeros((7, size * lines), f32)
        rate_f = consts["rate_f"]
        for chunk_at in range((near_filter + size - 1) // size):
            offset = chunk_at * size
            used = min(size, near_filter - offset)

            @pl.when(step == n_blocks + chunk_at)
            def _():
                spots = [(i, rate_f ** (offset + i - 2)) for i in range(used) if offset + i >= 2]
                qsum[0] = qsum[0] + weighted_rows(q_ref, spots)

            @pl.when(step == 2 * n_blocks - 1 - chunk_at)
            def _():
                spots = [
                    (size - 1 - i, rate_f ** (offset + i - 2)) for i in range(used) if offset + i >= 2
                ]
                qsum[1] = qsum[1] + weighted_rows(q_ref, spots)

        @pl.when(step == n_blocks)
        def _():
            xleft_ref[1] = q_ref[:, 0]
            xleft_ref[2] = q_ref[:, 1]

        @pl.when(step == 2 * n_blocks - 1)
        def _():
            xleft_ref[0] = qsum[0]
            xright_ref[0] = qsum[1]
            xright_ref[1] = q_ref[:, size - 1]
            xright_ref[2] = q_ref[:, size - 2]


def corner_body(xright_ref, xleft_ref, zl_ref, zr_ref, tr_ref, tl_ref, pz_ref, mask_ref, right_ref, left_ref):
    near = tr_ref.shape[0] // 3
    planes = jnp.concatenate([zl_ref[...], zr_ref[...]], axis=0)
    span = planes.shape[1]
    terms = right_ref.shape[0]
    lines = right_ref.shape[2]
    found = []
    for block, table in ((planes[:, span - near:], tr_ref), (planes[:, :near], tl_ref)):
        hi, lo = parts(block)
        found.append(dot(jnp.concatenate([hi, lo, hi], axis=1), table[...]))
    group = zl_ref.shape[0]
    both = jnp.concatenate(found, axis=1)
    columns = spread_columns(both[:group], both[group:])
    used = terms * lines
    columns = jnp.concatenate([columns[:used], columns[LANES:LANES + used]], axis=0)
    add = dot(jnp.concatenate([columns * mask_ref[comp] for comp in range(3)], axis=0), pz_ref[...])
    for comp in range(3):
        for term in range(terms):
            at = (2 * comp) * used + term * lines
            right_ref[term, comp] = xright_ref[term, comp] + add[at:at + lines]
            left_ref[term, comp] = xleft_ref[term, comp] + add[used + at:used + at + lines]


def filter_body(
    n_blocks, consts,
    q_ref, xl_ref, xr_ref, zl_ref, zr_ref, pz_ref, mask_ref,
    out_ref,
    full, back, adds, tail, lead,
):
    step = pl.program_id(0)
    size = q_ref.shape[1]
    count = q_ref.shape[3]
    lines = q_ref.shape[2]
    rate = consts["rate_f"]

    @pl.when(step == 0)
    def _():
        for k in range(3):
            tail[k] = xr_ref[k]
        full[n_blocks * size] = xr_ref[1]
        full[n_blocks * size + 1] = xr_ref[2]

    @pl.when(step < n_blocks)
    def _():
        base = (n_blocks - 1 - step) * size
        columns = spread_columns(zl_ref[...], zr_ref[...])
        masked = [columns * mask_ref[comp] for comp in range(3)]
        total, one, two = tail[0], tail[1], tail[2]
        sub = rows_sub
        for part in range(size // sub - 1, -1, -1):
            flat = slice(part * sub * lines, (part + 1) * sub * lines)
            edge = jnp.concatenate([masked[comp][flat] for comp in range(3)], axis=0)
            adds[:, part * sub:(part + 1) * sub] = dot(edge, pz_ref[...]).reshape(3, sub, lines, count)
        for i in range(size - 1, -1, -1):
            back[base + i] = total
            here = q_ref[:, i] + adds[:, i]
            full[base + i] = here
            total = rate * total + two
            two = one
            one = here
        tail[0] = total
        tail[1] = one
        tail[2] = two

    @pl.when(step == n_blocks)
    def _():
        for k in range(3):
            lead[k] = xl_ref[k]

    @pl.when(step >= n_blocks)
    def _():
        base = (step - n_blocks) * size
        total, one, two = lead[0], lead[1], lead[2]
        here = full[base]
        ahead = full[base + 1]
        for i in range(size):
            further = full[base + i + 2]
            value = (
                consts["k3"] * (total + back[base + i])
                + consts["k0"] * here
                + consts["k1"] * (ahead + one)
                + consts["k2"] * (further + two)
            )
            out_ref[:, i] = value
            total = rate * total + two
            two = one
            one = here
            here = ahead
            ahead = further
        lead[0] = total
        lead[1] = one
        lead[2] = two


def whole(shape):
    return pl.BlockSpec(shape, lambda t: (0,) * len(shape))


def in_hbm(values):
    return pltpu.with_memory_space_constraint(values, pltpu.HBM)


def ring(count, step):
    return [(i, (i + step) % count) for i in range(count)]


def swap(right, left, axis):
    count = lax.axis_size(axis)
    return (
        lax.ppermute(right, axis, ring(count, 1)),
        lax.ppermute(left, axis, ring(count, -1)),
    )


def shards(velocity, prior):
    comps, cells_x, lines, cells_z = velocity.shape
    spacing_x = 8.0 * math.pi / (cells_x * lax.axis_size("gx"))
    spacing_z = 3.0 * math.pi / (cells_z * lax.axis_size("gz"))
    dt_step = 0.3 / (1.0 / spacing_x + 1.0 / spacing_z)
    rate_d = decay_rate(alpha_deriv)
    rate_f = decay_rate(alpha_filter)
    size = rows_block
    n_blocks = cells_x // size
    span = cells_x * lines

    taps_x = deriv_taps(spacing_x)
    flat_part = taps_x[2] / alpha_deriv
    solve_part = (taps_x[1] - flat_part) * (-rate_d / alpha_deriv)
    kf = kernel_values([0, 1, 2, 3], filter_taps(), alpha_filter)
    consts = {
        "rate_d": rate_d,
        "ratio_d": flat_part / solve_part,
        "x_factor": -dt_step * solve_part,
        "rate_f": rate_f,
        "k0": float(kf[0]),
        "k1": float(kf[1]),
        "k2": float(kf[2]),
        "k3": float(kf[3]),
        "e0": float(5.0 / 12.0 * (kf[0] - kf[3] / rate_f**3)),
        "e1": float(5.0 / 12.0 * (kf[1] - kf[3] / rate_f**2)),
        "e2": float(5.0 / 12.0 * (kf[2] - kf[3] / rate_f)),
    }

    plane = (comps, lines, cells_z)
    big = lambda rows, idx: pl.BlockSpec((comps, rows, lines, cells_z), lambda t: (0, idx(t), 0, 0))
    thin = lambda group, rows, idx: pl.BlockSpec((group, rows * lines), lambda t: (0, idx(t)))
    edge = (2,) + plane
    group_d = 8
    taps_z = deriv_taps(spacing_z)
    cell = np.arange(near_deriv)
    weights = np.stack(
        [-dt_step * kernel_values(cell - near_deriv - term, taps_z, alpha_deriv) for term in range(2)]
        + [-dt_step * kernel_values(cell + 1 + term, taps_z, alpha_deriv) for term in range(2)]
    )
    weights = jnp.asarray(np.broadcast_to(weights[:, :, None], (4, near_deriv, LANES)), f32)
    zr_send, zl_send, xr_send, xl_send = pl.pallas_call(
        functools.partial(edge_body, rate_d),
        grid=(cells_x // rows_edge,),
        in_specs=[big(rows_edge, lambda t: t), whole(weights.shape)],
        out_specs=[thin(group_d, rows_edge, lambda t: t)] * 2 + [whole(edge)] * 2,
        out_shape=[jax.ShapeDtypeStruct((group_d, span), f32)] * 2
        + [jax.ShapeDtypeStruct(edge, f32)] * 2,
        name="edges",
        compiler_params=pltpu.CompilerParams(vmem_limit_bytes=12 << 20),
    )(in_hbm(velocity), in_hbm(weights))
    xl, xr = swap(xr_send, xl_send, "gx")
    zl, zr = swap(zr_send, zl_send, "gz")

    group_f = 16
    pd = padded_profiles(edge_profiles(cells_z, alpha_deriv, 2, group_d))
    dz = jnp.asarray(np.concatenate([band_matrix(cells_z, taps_z, alpha_deriv, -dt_step), pd], axis=0))
    mask_d = component_masks(2, group_d)
    fz = jnp.asarray(band_matrix(cells_z, filter_taps(), alpha_filter, 5.0 / 12.0))
    pf = jnp.asarray(padded_profiles(edge_profiles(cells_z, alpha_filter, 3, group_f)))
    mask_f = component_masks(3, group_f)
    later = lambda t: jnp.maximum(t - n_blocks, 0)
    early = lambda t: jnp.maximum(n_blocks - 1 - t, 0)
    turn = lambda t: jnp.where(t < n_blocks, n_blocks - 1 - t, t - n_blocks)
    edge3 = (3,) + plane
    block = (comps, size, lines, cells_z)
    advance, q, zr_send, zl_send, xr_part, xl_part = pl.pallas_call(
        functools.partial(advance_body, n_blocks, consts),
        grid=(2 * n_blocks,),
        in_specs=[
            big(size, turn), big(size, early), whole(edge), whole(edge),
            thin(group_d, size, early), thin(group_d, size, early),
            whole(dz.shape), whole(mask_d.shape), whole(fz.shape),
        ],
        out_specs=[
            big(size, later), big(size, later),
            thin(group_f, size, later), thin(group_f, size, later),
            whole(edge3), whole(edge3),
        ],
        out_shape=[
            jax.ShapeDtypeStruct(velocity.shape, f32),
            jax.ShapeDtypeStruct(velocity.shape, f32),
            jax.ShapeDtypeStruct((group_f, span), f32),
            jax.ShapeDtypeStruct((group_f, span), f32),
            jax.ShapeDtypeStruct(edge3, f32),
            jax.ShapeDtypeStruct(edge3, f32),
        ],
        scratch_shapes=[
            pltpu.VMEM((cells_x + 1,) + plane, f32),
            pltpu.VMEM((cells_x,) + plane, f32),
            pltpu.VMEM((n_blocks,) + block, f32),
            pltpu.VMEM((n_blocks + 1,) + plane, f32),
            pltpu.VMEM((comps, size * lines, cells_z), bf16),
            pltpu.VMEM((comps, size * lines, cells_z), bf16),
            pltpu.VMEM((comps, size * lines, LANES), f32),
            pltpu.VMEM(plane, f32),
            pltpu.VMEM((3,) + plane, f32),
            pltpu.VMEM((2,) + plane, f32),
        ],
        name="advance",
        compiler_params=pltpu.CompilerParams(vmem_limit_bytes=40 << 20),
    )(velocity, prior, xl, xr, zl, zr, in_hbm(dz), mask_d, in_hbm(fz))
    zl, zr = swap(zr_send, zl_send, "gz")

    near = near_filter * lines
    cell = np.arange(cells_x)[:, None, None, None]
    line = (np.arange(lines)[None, :, None, None] == np.arange(lines)[None, None, None, :]) * 1.0
    back_off = cells_x - 3 - cell
    grow = np.where(back_off >= 0, np.power(rate_f, np.maximum(back_off, 0)), 0.0)
    pick = np.concatenate([grow, cell == cells_x - 1, cell == cells_x - 2], axis=2) * 1.0
    right_table = (pick * line).reshape(span, 3 * lines)
    left_table = (pick[::-1] * line).reshape(span, 3 * lines)
    widen = lambda t: np.concatenate([t, np.zeros((near, 128 - t.shape[1]))], axis=1)
    triple = lambda t: jnp.asarray(np.concatenate([np_parts(t)[k] for k in (0, 0, 1)], axis=0))
    tr = triple(widen(right_table[span - near:]))
    tl = triple(widen(left_table[:near]))
    xr_send, xl_send = pl.pallas_call(
        corner_body,
        grid=(1,),
        in_specs=[
            whole(edge3), whole(edge3), whole((group_f, span)), whole((group_f, span)),
            whole(tr.shape), whole(tl.shape), whole(pf.shape), whole(mask_f.shape),
        ],
        out_specs=[whole(edge3)] * 2,
        out_shape=[jax.ShapeDtypeStruct(edge3, f32)] * 2,
        name="corner",
        compiler_params=pltpu.CompilerParams(vmem_limit_bytes=12 << 20),
    )(xr_part, xl_part, zl, zr, tr, tl, pf, mask_f)
    xl, xr = swap(xr_send, xl_send, "gx")

    n_parts = cells_x // rows_filter
    after = lambda t: jnp.maximum(t - n_parts, 0)
    before = lambda t: jnp.maximum(n_parts - 1 - t, 0)
    filtered = pl.pallas_call(
        functools.partial(filter_body, n_parts, consts),
        grid=(2 * n_parts,),
        in_specs=[
            big(rows_filter, before), whole(edge3), whole(edge3),
            thin(group_f, rows_filter, before), thin(group_f, rows_filter, before),
            whole(pf.shape), whole(mask_f.shape),
        ],
        out_specs=big(rows_filter, after),
        out_shape=jax.ShapeDtypeStruct(velocity.shape, f32),
        scratch_shapes=[
            pltpu.VMEM((cells_x + 2,) + plane, f32),
            pltpu.VMEM((cells_x,) + plane, f32),
            pltpu.VMEM((comps, rows_filter, lines, cells_z), f32),
            pltpu.VMEM((3,) + plane, f32),
            pltpu.VMEM((3,) + plane, f32),
        ],
        name="filter",
        compiler_params=pltpu.CompilerParams(vmem_limit_bytes=26 << 20),
    )(q, xl, xr, zl, zr, pf, mask_f)
    return (filtered, advance)


def solution(mesh):
    placed = P(None, "gx", None, "gz")
    return jax.shard_map(
        shards,
        mesh=mesh,
        in_specs=(placed, placed),
        out_specs=(placed, placed),
        check_vma=False,
    )
```

```python
import functools
import math

import jax
import jax.numpy as jnp
import numpy as np
from jax import lax
from jax.experimental import pallas as pl
from jax.experimental.pallas import tpu as pltpu
from jax.sharding import PartitionSpec as P

alpha_deriv = 1.0 / 3.0
alpha_filter = 0.49
rows_edge = 64
rows_block = 64
rows_sub = 16
rows_local = 16
rows_smooth = 16
limits = {"local": 8, "advance": 10, "smooth": 6, "carry": 5, "filter": 14}
rows_filter = 64
near_deriv = 32
near_filter = 96
LANES = 128
bf16 = jnp.bfloat16
f32 = jnp.float32


def decay_rate(alpha):
    return (-1.0 + math.sqrt(1.0 - 4.0 * alpha * alpha)) / (2.0 * alpha)


def green_scale(alpha):
    return 1.0 / (1.0 + 2.0 * alpha * decay_rate(alpha))


def kernel_values(offsets, taps, alpha):
    offsets = np.asarray(offsets, dtype=np.float64)
    total = np.zeros_like(offsets)
    for shift, weight in taps.items():
        total = total + weight * green_scale(alpha) * np.power(
            decay_rate(alpha), np.abs(offsets - shift)
        )
    return total


def deriv_taps(spacing):
    near = 14.0 / 9.0 / (2.0 * spacing)
    far = 1.0 / 9.0 / (4.0 * spacing)
    return {1: near, -1: -near, 2: far, -2: -far}


def filter_taps():
    taps = {0: (11.0 + 10.0 * alpha_filter) / 16.0}
    weights = (
        (15.0 + 34.0 * alpha_filter) / 32.0,
        (-3.0 + 6.0 * alpha_filter) / 16.0,
        (1.0 - 2.0 * alpha_filter) / 32.0,
    )
    for shift, weight in enumerate(weights, 1):
        taps[shift] = 0.5 * weight
        taps[-shift] = 0.5 * weight
    return taps


def parts(values):
    high = values.astype(bf16)
    low = (values - high.astype(f32)).astype(bf16)
    return high, low


def np_parts(values):
    values = np.asarray(values, dtype=np.float32)
    high = values.astype(bf16)
    low = (values - high.astype(np.float32)).astype(bf16)
    return high, low


def band_matrix(count, taps, alpha, factor):
    source = np.arange(count)[:, None]
    target = np.arange(count)[None, :]
    high, low = np_parts(factor * kernel_values(source - target, taps, alpha))
    return np.concatenate([high, high, low], axis=0)


def edge_profiles(count, alpha, terms, group):
    cell = np.arange(count)
    table = np.zeros((2 * group, count))
    rate = decay_rate(alpha)
    for term in range(terms):
        if term < terms - 1:
            shape = (cell == term) * 1.0
        else:
            shape = np.where(cell >= term, np.power(rate, np.maximum(cell - term, 0)), 0.0)
        for comp in range(3):
            table[term * 3 + comp] = shape
            table[group + term * 3 + comp] = shape[::-1]
    return table


def padded_profiles(table):
    high, low = np_parts(table)
    rest = np.zeros((LANES - 3 * table.shape[0], table.shape[1]), dtype=bf16)
    return np.concatenate([high, high, low, rest], axis=0)


def component_masks(terms, group):
    lane = np.arange(LANES)
    row = lane % group
    masks = [(lane < 6 * group) & (row < 3 * terms) & (row % 3 == comp) for comp in range(3)]
    return jnp.asarray(np.stack(masks)[:, None, :], bf16)


def spread_columns(left, right):
    both = jnp.concatenate([left, right], axis=0)
    high = both.astype(bf16).astype(f32)
    low = both - high
    rest = jnp.zeros((128 - 3 * both.shape[0], both.shape[1]), f32)
    return jnp.concatenate([high, low, high, rest], axis=0).T.astype(bf16)


def dot(a, b):
    return jnp.dot(a, b, preferred_element_type=f32)


def edge_body(rate, v_ref, weight_ref, zright_ref, zleft_ref, xright_ref, xleft_ref):
    step = pl.program_id(0)
    size, lines, count = v_ref.shape[1:]
    near = weight_ref.shape[1]
    group = LANES // lines
    left_lane = lax.broadcasted_iota(jnp.int32, (LANES, LANES), 1) < LANES // 2
    for comp in range(3):
        for part in range(size // group):
            block = v_ref[comp, part * group:(part + 1) * group].reshape(LANES, count)
            both = jnp.where(left_lane, block[:, :LANES], block[:, count - LANES:]).T
            span = slice(part * LANES, (part + 1) * LANES)
            for term in range(2):
                row = term * 3 + comp
                zright_ref[row:row + 1, span] = jnp.sum(
                    both[LANES - near:] * weight_ref[term], axis=0, keepdims=True
                )
                zleft_ref[row:row + 1, span] = jnp.sum(
                    both[:near] * weight_ref[2 + term], axis=0, keepdims=True
                )
    for row in range(6, 8):
        zright_ref[row:row + 1, :] = jnp.zeros((1, size * lines), f32)
        zleft_ref[row:row + 1, :] = jnp.zeros((1, size * lines), f32)

    @pl.when(step == 0)
    def _():
        total = v_ref[:, near_deriv - 1]
        for i in range(near_deriv - 2, -1, -1):
            total = rate * total + v_ref[:, i]
        xleft_ref[0] = total
        xleft_ref[1] = v_ref[:, 0]

    @pl.when(step == pl.num_programs(0) - 1)
    def _():
        total = v_ref[:, size - near_deriv]
        for i in range(size - near_deriv + 1, size):
            total = rate * total + v_ref[:, i]
        xright_ref[0] = total
        xright_ref[1] = v_ref[:, size - 1]


def weighted_rows(ref, weights):
    sums = [None] * 4
    for k, (row, weight) in enumerate(weights):
        term = weight * ref[:, row]
        sums[k % 4] = term if sums[k % 4] is None else sums[k % 4] + term
    return (sums[0] + sums[1]) + (sums[2] + sums[3])


def rows_of(ref, chunk, size):
    return ref.at[:, pl.ds(chunk * size, size)]


def local_body(
    n_blocks, consts, v_all, prior_ref, dz_ref, slope_all, back_all, base_all, heads_ref, tail
):
    step = pl.program_id(0)
    size, lines, count = prior_ref.shape[1:]
    rate = consts["rate_d"]
    chunk = n_blocks - 1 - step
    v_ref, slope_ref, back_ref, base_ref = [
        rows_of(ref, chunk, size) for ref in (v_all, slope_all, back_all, base_all)
    ]

    @pl.when(step == 0)
    def _():
        tail[...] = jnp.zeros_like(tail)

    sub = rows_local
    total = tail[...]
    for part in range(size // sub - 1, -1, -1):
        rows = slice(part * sub, (part + 1) * sub)
        hi, lo = parts(v_ref[:, rows].reshape(3 * sub * lines, count))
        lhs = jnp.concatenate([hi, lo, hi], axis=1)
        slope_ref[:, rows] = dot(lhs, dz_ref[...]).reshape(3, sub, lines, count)
        for i in range((part + 1) * sub - 1, part * sub - 1, -1):
            here = v_ref[:, i]
            total = here + rate * total
            back_ref[:, i] = total
            base_ref[:, i] = 2.4 * here - 0.68 * prior_ref[:, i]
    tail[...] = total
    heads_ref[chunk, 0] = total
    heads_ref[chunk, 1] = v_ref[:, 0]


def advance_body(
    n_blocks, consts,
    v_all, slope_all, back_all, base_all, heads_ref, xl_ref, xr_ref, zl_ref, zr_ref,
    pz_ref, mask_ref, weight_ref,
    adv_ref, prov_all, zright_ref, zleft_ref,
    extra, lead,
):
    step = pl.program_id(0)
    size, lines, count = adv_ref.shape[1:]
    v_ref, slope_ref, back_ref, base_ref, prov_ref = [
        rows_of(ref, step, size) for ref in (v_all, slope_all, back_all, base_all, prov_all)
    ]
    sub = rows_sub
    rate = consts["rate_d"]
    ratio = consts["ratio_d"]
    near = weight_ref.shape[1]

    @pl.when(step == 0)
    def _():
        before = (xl_ref[0] + rate * back_ref[:, 0]) * (1.0 / (1.0 - rate * rate))
        value = back_ref[:, 0] + rate * before
        lead[0] = value
        lead[1] = before + ratio * xl_ref[1]
        lead[2] = value + ratio * v_ref[:, 0]

    columns = spread_columns(zl_ref[...], zr_ref[...])
    edge = jnp.concatenate([columns * mask_ref[comp] for comp in range(3)], axis=0)
    extra[...] = dot(edge, pz_ref[...]).reshape(3, size, lines, count)
    last = step == n_blocks - 1
    following = jnp.minimum(step + 1, n_blocks - 1)
    beyond = jnp.where(last, xr_ref[0], 0.0)
    back_next = jnp.where(last, xr_ref[0], heads_ref[following, 0])
    here_next = jnp.where(last, xr_ref[1], heads_ref[following, 1])
    value, behind, level = lead[0], lead[1], lead[2]
    here = v_ref[:, 0]
    for part in range(size // sub):
        for i in range(part * sub, (part + 1) * sub):
            if i + 1 < size:
                ahead = v_ref[:, i + 1]
                back = back_ref[:, i + 1]
                if size - 1 - i <= near_deriv:
                    back = back + (rate ** (size - 1 - i)) * beyond
            else:
                ahead = here_next
                back = back_next
            value = back + rate * value
            above = value + ratio * ahead
            gx = above - behind
            behind = level
            level = above
            ux = consts["x_factor"] * here[0]
            adv = ux[None] * gx + here[2][None] * (slope_ref[:, i] + extra[:, i])
            adv_ref[:, i] = adv
            prov_ref[:, i] = base_ref[:, i] + adv
            here = ahead
        for comp in range(3):
            for piece in range(sub * lines // LANES):
                first = part * sub + piece * (LANES // lines)
                tile = prov_ref[comp, first:first + LANES // lines].reshape(LANES, count)
                lanes = slice(first * lines, first * lines + LANES)
                right = tile[:, count - LANES:].T
                left = tile[:, :LANES].T
                for ref, near_part, f0, f1, weight in (
                    (zright_ref, right[LANES - near:], right[127:128], right[126:127], weight_ref[0]),
                    (zleft_ref, left[:near], left[0:1], left[1:2], weight_ref[1]),
                ):
                    cs = consts["e3"] * jnp.sum(near_part * weight, axis=0, keepdims=True)
                    r = consts["rate_f"]
                    ref[comp:comp + 1, lanes] = r * cs + consts["e1"] * f0 + consts["e2"] * f1
                    ref[3 + comp:4 + comp, lanes] = (r * r) * cs + consts["e2"] * f0
                    ref[6 + comp:7 + comp, lanes] = (r * r * r) * cs
    lead[0] = value
    lead[1] = behind
    lead[2] = level
    for ref in (zright_ref, zleft_ref):
        ref[9:16, :] = jnp.zeros((7, size * lines), f32)


def smooth_body(n_blocks, consts, prov_all, fz_ref, q_all, xright_ref, xleft_ref, qsum):
    step = pl.program_id(0)
    cells, lines, count = prov_all.shape[1:]
    size = cells // n_blocks
    prov_ref, q_ref = [rows_of(ref, step, size) for ref in (prov_all, q_all)]
    rate = consts["rate_f"]

    @pl.when(step == 0)
    def _():
        qsum[...] = jnp.zeros_like(qsum)

    sub = rows_smooth
    for part in range(size // sub):
        rows = slice(part * sub, (part + 1) * sub)
        hi, lo = parts(prov_ref[:, rows].reshape(3 * sub * lines, count))
        lhs = jnp.concatenate([hi, lo, hi], axis=1)
        q_ref[:, rows] = dot(lhs, fz_ref[...]).reshape(3, sub, lines, count)
    for chunk_at in range((near_filter + size - 1) // size):
        offset = chunk_at * size
        used = min(size, near_filter - offset)

        @pl.when(step == chunk_at)
        def _():
            spots = [(i, rate ** (offset + i - 2)) for i in range(used) if offset + i >= 2]
            qsum[0] = qsum[0] + weighted_rows(q_ref, spots)

        @pl.when(step == n_blocks - 1 - chunk_at)
        def _():
            spots = [(size - 1 - i, rate ** (offset + i - 2)) for i in range(used) if offset + i >= 2]
            qsum[1] = qsum[1] + weighted_rows(q_ref, spots)

    @pl.when(step == 0)
    def _():
        xleft_ref[1] = q_ref[:, 0]
        xleft_ref[2] = q_ref[:, 1]

    @pl.when(step == n_blocks - 1)
    def _():
        xleft_ref[0] = qsum[0]
        xright_ref[0] = qsum[1]
        xright_ref[1] = q_ref[:, size - 1]
        xright_ref[2] = q_ref[:, size - 2]


def carry_body(n_blocks, q_all, zl_ref, zr_ref, pz_ref, mask_ref, full_all):
    cells, lines, count = q_all.shape[1:]
    size = cells // n_blocks
    q_ref, full_ref = [rows_of(ref, pl.program_id(0), size) for ref in (q_all, full_all)]
    columns = spread_columns(zl_ref[...], zr_ref[...])
    edge = jnp.concatenate([columns * mask_ref[comp] for comp in range(3)], axis=0)
    full_ref[...] = q_ref[...] + dot(edge, pz_ref[...]).reshape(3, size, lines, count)


def corner_body(xright_ref, xleft_ref, zl_ref, zr_ref, tr_ref, tl_ref, pz_ref, mask_ref, right_ref, left_ref):
    near = tr_ref.shape[0] // 3
    planes = jnp.concatenate([zl_ref[...], zr_ref[...]], axis=0)
    span = planes.shape[1]
    terms = right_ref.shape[0]
    lines = right_ref.shape[2]
    found = []
    for block, table in ((planes[:, span - near:], tr_ref), (planes[:, :near], tl_ref)):
        hi, lo = parts(block)
        found.append(dot(jnp.concatenate([hi, lo, hi], axis=1), table[...]))
    group = zl_ref.shape[0]
    both = jnp.concatenate(found, axis=1)
    columns = spread_columns(both[:group], both[group:])
    used = terms * lines
    columns = jnp.concatenate([columns[:used], columns[LANES:LANES + used]], axis=0)
    add = dot(jnp.concatenate([columns * mask_ref[comp] for comp in range(3)], axis=0), pz_ref[...])
    for comp in range(3):
        for term in range(terms):
            at = (2 * comp) * used + term * lines
            right_ref[term, comp] = xright_ref[term, comp] + add[at:at + lines]
            left_ref[term, comp] = xleft_ref[term, comp] + add[used + at:used + at + lines]


def filter_body(n_blocks, consts, q_all, xl_ref, xr_ref, out_ref, back, heads, tail, lead):
    step = pl.program_id(0)
    size = out_ref.shape[1]
    q_ref = rows_of(q_all, jnp.where(step < n_blocks, n_blocks - 1 - step, step - n_blocks), size)
    rate = consts["rate_f"]

    @pl.when(step == 0)
    def _():
        for k in range(3):
            tail[k] = xr_ref[k]
        heads[n_blocks, 0] = xr_ref[1]
        heads[n_blocks, 1] = xr_ref[2]

    @pl.when(step < n_blocks)
    def _():
        chunk = n_blocks - 1 - step
        base = chunk * size
        total, one, two = tail[0], tail[1], tail[2]
        for i in range(size - 1, -1, -1):
            back[base + i] = total
            total = rate * total + two
            two = one
            one = q_ref[:, i]
        tail[0] = total
        tail[1] = one
        tail[2] = two
        heads[chunk, 0] = one
        heads[chunk, 1] = two

    @pl.when(step == n_blocks)
    def _():
        for k in range(3):
            lead[k] = xl_ref[k]

    @pl.when(step >= n_blocks)
    def _():
        chunk = step - n_blocks
        base = chunk * size
        total, one, two = lead[0], lead[1], lead[2]
        here = q_ref[:, 0]
        ahead = q_ref[:, 1]
        for i in range(size):
            further = q_ref[:, i + 2] if i + 2 < size else heads[chunk + 1, i + 2 - size]
            value = (
                consts["k3"] * (total + back[base + i])
                + consts["k0"] * here
                + consts["k1"] * (ahead + one)
                + consts["k2"] * (further + two)
            )
            out_ref[:, i] = value
            total = rate * total + two
            two = one
            one = here
            here = ahead
            ahead = further
        lead[0] = total
        lead[1] = one
        lead[2] = two


def whole(shape):
    return pl.BlockSpec(shape, lambda t: (0,) * len(shape))


def in_hbm(values):
    return pltpu.with_memory_space_constraint(values, pltpu.HBM)


def ring(count, step):
    return [(i, (i + step) % count) for i in range(count)]


def swap(right, left, axis):
    count = lax.axis_size(axis)
    return (
        lax.ppermute(right, axis, ring(count, 1)),
        lax.ppermute(left, axis, ring(count, -1)),
    )


def shards(velocity, prior):
    comps, cells_x, lines, cells_z = velocity.shape
    spacing_x = 8.0 * math.pi / (cells_x * lax.axis_size("gx"))
    spacing_z = 3.0 * math.pi / (cells_z * lax.axis_size("gz"))
    dt_step = 0.3 / (1.0 / spacing_x + 1.0 / spacing_z)
    rate_d = decay_rate(alpha_deriv)
    rate_f = decay_rate(alpha_filter)
    size = rows_block
    n_blocks = cells_x // size
    span = cells_x * lines

    taps_x = deriv_taps(spacing_x)
    flat_part = taps_x[2] / alpha_deriv
    solve_part = (taps_x[1] - flat_part) * (-rate_d / alpha_deriv)
    kf = kernel_values([0, 1, 2, 3], filter_taps(), alpha_filter)
    consts = {
        "rate_d": rate_d,
        "ratio_d": flat_part / solve_part,
        "x_factor": -dt_step * solve_part,
        "rate_f": rate_f,
        "k0": float(kf[0]),
        "k1": float(kf[1]),
        "k2": float(kf[2]),
        "k3": float(kf[3]),
        "e3": float(5.0 / 12.0 * kf[3] / rate_f**3),
        "e1": float(5.0 / 12.0 * (kf[1] - kf[3] / rate_f**2)),
        "e2": float(5.0 / 12.0 * (kf[2] - kf[3] / rate_f)),
    }

    plane = (comps, lines, cells_z)
    big = lambda rows, idx: pl.BlockSpec((comps, rows, lines, cells_z), lambda t: (0, idx(t), 0, 0))
    thin = lambda group, rows, idx: pl.BlockSpec((group, rows * lines), lambda t: (0, idx(t)))
    edge = (2,) + plane
    group_d = 8
    taps_z = deriv_taps(spacing_z)
    cell = np.arange(near_deriv)
    weights = np.stack(
        [-dt_step * kernel_values(cell - near_deriv - term, taps_z, alpha_deriv) for term in range(2)]
        + [-dt_step * kernel_values(cell + 1 + term, taps_z, alpha_deriv) for term in range(2)]
    )
    weights = jnp.asarray(np.broadcast_to(weights[:, :, None], (4, near_deriv, LANES)), f32)
    zr_send, zl_send, xr_send, xl_send = pl.pallas_call(
        functools.partial(edge_body, rate_d),
        grid=(cells_x // rows_edge,),
        in_specs=[big(rows_edge, lambda t: t), whole(weights.shape)],
        out_specs=[thin(group_d, rows_edge, lambda t: t)] * 2 + [whole(edge)] * 2,
        out_shape=[jax.ShapeDtypeStruct((group_d, span), f32)] * 2
        + [jax.ShapeDtypeStruct(edge, f32)] * 2,
        name="edges",
        compiler_params=pltpu.CompilerParams(vmem_limit_bytes=8 << 20),
    )(in_hbm(velocity), in_hbm(weights))
    xl, xr = swap(xr_send, xl_send, "gx")
    zl, zr = swap(zr_send, zl_send, "gz")

    group_f = 16
    plain = lambda t: t
    held = pl.BlockSpec(memory_space=pltpu.VMEM)
    edge3 = (3,) + plane
    block = (comps, size, lines, cells_z)
    field = jax.ShapeDtypeStruct(velocity.shape, f32)
    dz = jnp.asarray(band_matrix(cells_z, taps_z, alpha_deriv, -dt_step))
    heads_shape = (n_blocks, 2) + plane
    reverse = lambda t: n_blocks - 1 - t
    slope, back, base, heads = pl.pallas_call(
        functools.partial(local_body, n_blocks, consts),
        grid=(n_blocks,),
        in_specs=[held, big(size, reverse), whole(dz.shape)],
        out_specs=[held, held, held, whole(heads_shape)],
        out_shape=[field] * 3 + [jax.ShapeDtypeStruct(heads_shape, f32)],
        scratch_shapes=[pltpu.VMEM(plane, f32)],
        name="local",
        compiler_params=pltpu.CompilerParams(vmem_limit_bytes=limits["local"] << 20),
        cost_estimate=pl.CostEstimate(flops=2 * 6144 * 768 * 256, bytes_accessed=25 << 20, transcendentals=0),
    )(velocity, in_hbm(prior), in_hbm(dz))

    pd = jnp.asarray(padded_profiles(edge_profiles(cells_z, alpha_deriv, 2, group_d)))
    mask_d = component_masks(2, group_d)
    decay = np.power(rate_f, np.arange(near_filter))
    decay = np.stack([decay[::-1], decay])
    decay = jnp.asarray(np.broadcast_to(decay[:, :, None], (2, near_filter, LANES)), f32)
    advance, prov, zr_send, zl_send = pl.pallas_call(
        functools.partial(advance_body, n_blocks, consts),
        grid=(n_blocks,),
        in_specs=[held, held, held, held] + [
            whole(heads_shape), whole(edge), whole(edge),
            thin(group_d, size, plain), thin(group_d, size, plain),
            whole(pd.shape), whole(mask_d.shape), whole(decay.shape),
        ],
        out_specs=[big(size, plain), held] + [thin(group_f, size, plain)] * 2,
        out_shape=[field] * 2 + [jax.ShapeDtypeStruct((group_f, span), f32)] * 2,
        scratch_shapes=[pltpu.VMEM(block, f32), pltpu.VMEM((3,) + plane, f32)],
        name="advance",
        compiler_params=pltpu.CompilerParams(vmem_limit_bytes=limits["advance"] << 20),
    )(velocity, slope, back, base, heads, xl, xr, zl, zr, pd, mask_d, decay)
    zl, zr = swap(zr_send, zl_send, "gz")

    fz = jnp.asarray(band_matrix(cells_z, filter_taps(), alpha_filter, 5.0 / 12.0))
    pf = jnp.asarray(padded_profiles(edge_profiles(cells_z, alpha_filter, 3, group_f)))
    mask_f = component_masks(3, group_f)
    q, xr_part, xl_part = pl.pallas_call(
        functools.partial(smooth_body, n_blocks, consts),
        grid=(n_blocks,),
        in_specs=[held, whole(fz.shape)],
        out_specs=[held, whole(edge3), whole(edge3)],
        out_shape=[field] + [jax.ShapeDtypeStruct(edge3, f32)] * 2,
        scratch_shapes=[pltpu.VMEM((2,) + plane, f32)],
        name="smooth",
        compiler_params=pltpu.CompilerParams(vmem_limit_bytes=limits["smooth"] << 20),
        cost_estimate=pl.CostEstimate(flops=2 * 6144 * 768 * 256, bytes_accessed=12 << 20, transcendentals=0),
    )(prov, in_hbm(fz))

    near = near_filter * lines
    cell = np.arange(cells_x)[:, None, None, None]
    line = (np.arange(lines)[None, :, None, None] == np.arange(lines)[None, None, None, :]) * 1.0
    back_off = cells_x - 3 - cell
    grow = np.where(back_off >= 0, np.power(rate_f, np.maximum(back_off, 0)), 0.0)
    pick = np.concatenate([grow, cell == cells_x - 1, cell == cells_x - 2], axis=2) * 1.0
    right_table = (pick * line).reshape(span, 3 * lines)
    left_table = (pick[::-1] * line).reshape(span, 3 * lines)
    widen = lambda t: np.concatenate([t, np.zeros((near, 128 - t.shape[1]))], axis=1)
    triple = lambda t: jnp.asarray(np.concatenate([np_parts(t)[k] for k in (0, 0, 1)], axis=0))
    tr = triple(widen(right_table[span - near:]))
    tl = triple(widen(left_table[:near]))
    xr_send, xl_send = pl.pallas_call(
        corner_body,
        grid=(1,),
        in_specs=[
            whole(edge3), whole(edge3), whole((group_f, span)), whole((group_f, span)),
            whole(tr.shape), whole(tl.shape), whole(pf.shape), whole(mask_f.shape),
        ],
        out_specs=[whole(edge3)] * 2,
        out_shape=[jax.ShapeDtypeStruct(edge3, f32)] * 2,
        name="corner",
        compiler_params=pltpu.CompilerParams(vmem_limit_bytes=8 << 20),
    )(xr_part, xl_part, zl, zr, tr, tl, pf, mask_f)
    xl, xr = swap(xr_send, xl_send, "gx")

    n_parts = cells_x // rows_filter
    after = lambda t: jnp.maximum(t - n_parts, 0)
    q = pl.pallas_call(
        functools.partial(carry_body, n_parts),
        grid=(n_parts,),
        in_specs=[
            held, thin(group_f, rows_filter, plain), thin(group_f, rows_filter, plain),
            whole(pf.shape), whole(mask_f.shape),
        ],
        out_specs=held,
        out_shape=field,
        name="carry",
        compiler_params=pltpu.CompilerParams(vmem_limit_bytes=limits["carry"] << 20),
        cost_estimate=pl.CostEstimate(flops=2 * 6144 * 128 * 256, bytes_accessed=12 << 20, transcendentals=0),
    )(q, zl, zr, pf, mask_f)
    filtered = pl.pallas_call(
        functools.partial(filter_body, n_parts, consts),
        grid=(2 * n_parts,),
        in_specs=[held, whole(edge3), whole(edge3)],
        out_specs=big(rows_filter, after),
        out_shape=field,
        scratch_shapes=[
            pltpu.VMEM((cells_x,) + plane, f32),
            pltpu.VMEM((n_parts + 1, 2) + plane, f32),
            pltpu.VMEM((3,) + plane, f32),
            pltpu.VMEM((3,) + plane, f32),
        ],
        name="filter",
        compiler_params=pltpu.CompilerParams(vmem_limit_bytes=limits["filter"] << 20),
    )(q, xl, xr)
    return (filtered, advance)


def solution(mesh):
    placed = P(None, "gx", None, "gz")
    return jax.shard_map(
        shards,
        mesh=mesh,
        in_specs=(placed, placed),
        out_specs=(placed, placed),
        check_vma=False,
    )
```

```python
import functools
import math

import jax
import jax.numpy as jnp
import numpy as np
from jax import lax
from jax.experimental import pallas as pl
from jax.experimental.pallas import tpu as pltpu
from jax.sharding import PartitionSpec as P

alpha_deriv = 1.0 / 3.0
alpha_filter = 0.49
rows_edge = 64
rows_block = 64
rows_sub = 64
rows_local = 8
rows_smooth = 16
rows_carry = 16
limits = {"edges": 6, "local": 8, "advance": 10, "smooth": 6, "carry": 5, "filter": 8}
rows_filter = 64
near_deriv = 32
near_filter = 96
LANES = 128
bf16 = jnp.bfloat16
f32 = jnp.float32


def decay_rate(alpha):
    return (-1.0 + math.sqrt(1.0 - 4.0 * alpha * alpha)) / (2.0 * alpha)


def green_scale(alpha):
    return 1.0 / (1.0 + 2.0 * alpha * decay_rate(alpha))


def kernel_values(offsets, taps, alpha):
    offsets = np.asarray(offsets, dtype=np.float64)
    total = np.zeros_like(offsets)
    for shift, weight in taps.items():
        total = total + weight * green_scale(alpha) * np.power(
            decay_rate(alpha), np.abs(offsets - shift)
        )
    return total


def deriv_taps(spacing):
    near = 14.0 / 9.0 / (2.0 * spacing)
    far = 1.0 / 9.0 / (4.0 * spacing)
    return {1: near, -1: -near, 2: far, -2: -far}


def filter_taps():
    taps = {0: (11.0 + 10.0 * alpha_filter) / 16.0}
    weights = (
        (15.0 + 34.0 * alpha_filter) / 32.0,
        (-3.0 + 6.0 * alpha_filter) / 16.0,
        (1.0 - 2.0 * alpha_filter) / 32.0,
    )
    for shift, weight in enumerate(weights, 1):
        taps[shift] = 0.5 * weight
        taps[-shift] = 0.5 * weight
    return taps


def parts(values):
    high = values.astype(bf16)
    low = (values - high.astype(f32)).astype(bf16)
    return high, low


def np_parts(values):
    values = np.asarray(values, dtype=np.float32)
    high = values.astype(bf16)
    low = (values - high.astype(np.float32)).astype(bf16)
    return high, low


def band_matrix(count, taps, alpha, factor):
    source = np.arange(count)[:, None]
    target = np.arange(count)[None, :]
    high, low = np_parts(factor * kernel_values(source - target, taps, alpha))
    return np.concatenate([high, high, low], axis=0)


def edge_profiles(count, alpha, terms, group):
    cell = np.arange(count)
    table = np.zeros((2 * group, count))
    rate = decay_rate(alpha)
    for term in range(terms):
        if term < terms - 1:
            shape = (cell == term) * 1.0
        else:
            shape = np.where(cell >= term, np.power(rate, np.maximum(cell - term, 0)), 0.0)
        for comp in range(3):
            table[term * 3 + comp] = shape
            table[group + term * 3 + comp] = shape[::-1]
    return table


def padded_profiles(table):
    high, low = np_parts(table)
    rest = np.zeros((LANES - 3 * table.shape[0], table.shape[1]), dtype=bf16)
    return np.concatenate([high, high, low, rest], axis=0)


def component_masks(terms, group):
    lane = np.arange(LANES)
    row = lane % group
    masks = [(lane < 6 * group) & (row < 3 * terms) & (row % 3 == comp) for comp in range(3)]
    return jnp.asarray(np.stack(masks)[:, None, :], bf16)


def spread_columns(left, right):
    both = jnp.concatenate([left, right], axis=0)
    high = both.astype(bf16).astype(f32)
    low = both - high
    rest = jnp.zeros((128 - 3 * both.shape[0], both.shape[1]), f32)
    return jnp.concatenate([high, low, high, rest], axis=0).T.astype(bf16)


def dot(a, b):
    return jnp.dot(a, b, preferred_element_type=f32)


def rows_of(ref, chunk, size):
    return ref.at[:, pl.ds(chunk * size, size)]


def edge_body(
    rate, n_blocks,
    v_hbm, weight_ref, table_hbm,
    zright_ref, zleft_ref, xright_ref, xleft_ref, v_all, table_ref,
    sems,
):
    step = pl.program_id(0)
    cells, lines, count = v_all.shape[1:]
    size = cells // n_blocks

    def fetch(chunk):
        rows = pl.ds(chunk * size, size)
        return pltpu.make_async_copy(v_hbm.at[:, rows], v_all.at[:, rows], sems.at[chunk])

    table = pltpu.make_async_copy(table_hbm, table_ref, sems.at[n_blocks])

    @pl.when(step == 0)
    def _():
        for chunk in range(n_blocks):
            fetch(chunk).start()
        table.start()

    fetch(step).wait()
    v_ref = rows_of(v_all, step, size)
    near = weight_ref.shape[1]
    group = LANES // lines
    left_lane = lax.broadcasted_iota(jnp.int32, (LANES, LANES), 1) < LANES // 2
    for comp in range(3):
        for part in range(size // group):
            block = v_ref[comp, part * group:(part + 1) * group].reshape(LANES, count)
            both = jnp.where(left_lane, block[:, :LANES], block[:, count - LANES:]).T
            span = slice(part * LANES, (part + 1) * LANES)
            for term in range(2):
                row = term * 3 + comp
                zright_ref[row:row + 1, span] = jnp.sum(
                    both[LANES - near:] * weight_ref[term], axis=0, keepdims=True
                )
                zleft_ref[row:row + 1, span] = jnp.sum(
                    both[:near] * weight_ref[2 + term], axis=0, keepdims=True
                )
    for row in range(6, 8):
        zright_ref[row:row + 1, :] = jnp.zeros((1, size * lines), f32)
        zleft_ref[row:row + 1, :] = jnp.zeros((1, size * lines), f32)

    @pl.when(step == 0)
    def _():
        total = v_ref[:, near_deriv - 1]
        for i in range(near_deriv - 2, -1, -1):
            total = rate * total + v_ref[:, i]
        xleft_ref[0] = total
        xleft_ref[1] = v_ref[:, 0]

    @pl.when(step == pl.num_programs(0) - 1)
    def _():
        total = v_ref[:, size - near_deriv]
        for i in range(size - near_deriv + 1, size):
            total = rate * total + v_ref[:, i]
        xright_ref[0] = total
        xright_ref[1] = v_ref[:, size - 1]
        table.wait()


def weighted_rows(ref, weights):
    sums = [None] * 4
    for k, (row, weight) in enumerate(weights):
        term = weight * ref[:, row]
        sums[k % 4] = term if sums[k % 4] is None else sums[k % 4] + term
    return (sums[0] + sums[1]) + (sums[2] + sums[3])


def local_body(
    n_blocks, consts, v_all, prior_all, dz_ref, slope_all, back_all, base_all, heads_ref, tail
):
    step = pl.program_id(0)
    cells, lines, count = v_all.shape[1:]
    size = cells // n_blocks
    rate = consts["rate_d"]
    chunk = n_blocks - 1 - step
    v_ref, prior_ref, slope_ref, back_ref, base_ref = [
        rows_of(ref, chunk, size) for ref in (v_all, prior_all, slope_all, back_all, base_all)
    ]

    @pl.when(step == 0)
    def _():
        tail[...] = jnp.zeros_like(tail)

    sub = rows_local
    total = tail[...]
    for part in range(size // sub - 1, -1, -1):
        rows = slice(part * sub, (part + 1) * sub)
        hi, lo = parts(v_ref[:, rows].reshape(3 * sub * lines, count))
        lhs = jnp.concatenate([hi, lo, hi], axis=1)
        slope_ref[:, rows] = dot(lhs, dz_ref[...]).reshape(3, sub, lines, count)
        for i in range((part + 1) * sub - 1, part * sub - 1, -1):
            here = v_ref[:, i]
            total = here + rate * total
            back_ref[:, i] = total
            base_ref[:, i] = 2.4 * here - 0.68 * prior_ref[:, i]
    tail[...] = total
    heads_ref[chunk, 0] = total
    heads_ref[chunk, 1] = v_ref[:, 0]


def advance_body(
    n_blocks, consts,
    v_all, slope_all, back_all, base_all, heads_ref, xl_ref, xr_ref, zl_ref, zr_ref,
    pz_ref, mask_ref, weight_ref,
    adv_ref, prov_all, zright_ref, zleft_ref,
    extra, lead,
):
    step = pl.program_id(0)
    size, lines, count = adv_ref.shape[1:]
    v_ref, slope_ref, back_ref, base_ref, prov_ref = [
        rows_of(ref, step, size) for ref in (v_all, slope_all, back_all, base_all, prov_all)
    ]
    sub = rows_sub
    rate = consts["rate_d"]
    ratio = consts["ratio_d"]
    near = weight_ref.shape[1]

    @pl.when(step == 0)
    def _():
        before = (xl_ref[0] + rate * back_ref[:, 0]) * (1.0 / (1.0 - rate * rate))
        value = back_ref[:, 0] + rate * before
        lead[0] = value
        lead[1] = before + ratio * xl_ref[1]
        lead[2] = value + ratio * v_ref[:, 0]

    columns = spread_columns(zl_ref[...], zr_ref[...])
    edge = jnp.concatenate([columns * mask_ref[comp] for comp in range(3)], axis=0)
    extra[...] = dot(edge, pz_ref[...]).reshape(3, size, lines, count)
    last = step == n_blocks - 1
    following = jnp.minimum(step + 1, n_blocks - 1)
    beyond = jnp.where(last, xr_ref[0], 0.0)
    back_next = jnp.where(last, xr_ref[0], heads_ref[following, 0])
    here_next = jnp.where(last, xr_ref[1], heads_ref[following, 1])
    value, behind, level = lead[0], lead[1], lead[2]
    here = v_ref[:, 0]
    for part in range(size // sub):
        for i in range(part * sub, (part + 1) * sub):
            if i + 1 < size:
                ahead = v_ref[:, i + 1]
                back = back_ref[:, i + 1]
                if size - 1 - i <= near_deriv:
                    back = back + (rate ** (size - 1 - i)) * beyond
            else:
                ahead = here_next
                back = back_next
            value = back + rate * value
            above = value + ratio * ahead
            gx = above - behind
            behind = level
            level = above
            ux = consts["x_factor"] * here[0]
            adv = ux[None] * gx + here[2][None] * (slope_ref[:, i] + extra[:, i])
            adv_ref[:, i] = adv
            prov_ref[:, i] = base_ref[:, i] + adv
            here = ahead
        for comp in range(3):
            for piece in range(sub * lines // LANES):
                first = part * sub + piece * (LANES // lines)
                tile = prov_ref[comp, first:first + LANES // lines].reshape(LANES, count)
                lanes = slice(first * lines, first * lines + LANES)
                right = tile[:, count - LANES:].T
                left = tile[:, :LANES].T
                for ref, near_part, f0, f1, weight in (
                    (zright_ref, right[LANES - near:], right[127:128], right[126:127], weight_ref[0]),
                    (zleft_ref, left[:near], left[0:1], left[1:2], weight_ref[1]),
                ):
                    cs = consts["e3"] * jnp.sum(near_part * weight, axis=0, keepdims=True)
                    r = consts["rate_f"]
                    ref[comp:comp + 1, lanes] = r * cs + consts["e1"] * f0 + consts["e2"] * f1
                    ref[3 + comp:4 + comp, lanes] = (r * r) * cs + consts["e2"] * f0
                    ref[6 + comp:7 + comp, lanes] = (r * r * r) * cs
    lead[0] = value
    lead[1] = behind
    lead[2] = level
    for ref in (zright_ref, zleft_ref):
        ref[9:16, :] = jnp.zeros((7, size * lines), f32)


def smooth_body(n_blocks, consts, prov_all, fz_ref, q_all, xright_ref, xleft_ref, qsum):
    step = pl.program_id(0)
    cells, lines, count = prov_all.shape[1:]
    size = cells // n_blocks
    prov_ref, q_ref = [rows_of(ref, step, size) for ref in (prov_all, q_all)]
    rate = consts["rate_f"]

    @pl.when(step == 0)
    def _():
        qsum[...] = jnp.zeros_like(qsum)

    sub = rows_smooth
    for part in range(size // sub):
        rows = slice(part * sub, (part + 1) * sub)
        hi, lo = parts(prov_ref[:, rows].reshape(3 * sub * lines, count))
        lhs = jnp.concatenate([hi, lo, hi], axis=1)
        q_ref[:, rows] = dot(lhs, fz_ref[...]).reshape(3, sub, lines, count)
    for chunk_at in range((near_filter + size - 1) // size):
        offset = chunk_at * size
        used = min(size, near_filter - offset)

        @pl.when(step == chunk_at)
        def _():
            spots = [(i, rate ** (offset + i)) for i in range(used)]
            qsum[0] = qsum[0] + weighted_rows(q_ref, spots)

        @pl.when(step == n_blocks - 1 - chunk_at)
        def _():
            spots = [(size - 1 - i, rate ** (offset + i)) for i in range(used)]
            qsum[1] = qsum[1] + weighted_rows(q_ref, spots)

    @pl.when(step == 0)
    def _():
        xleft_ref[1] = q_ref[:, 0]
        xleft_ref[2] = q_ref[:, 1]

    @pl.when(step == n_blocks - 1)
    def _():
        xleft_ref[0] = qsum[0]
        xright_ref[0] = qsum[1]
        xright_ref[1] = q_ref[:, size - 1]
        xright_ref[2] = q_ref[:, size - 2]


def carry_body(n_blocks, rate, q_all, zl_ref, zr_ref, pz_ref, mask_ref, full_all, back_all, tail):
    step = pl.program_id(0)
    cells, lines, count = q_all.shape[1:]
    size = cells // n_blocks
    chunk = n_blocks - 1 - step
    q_ref, full_ref, back_ref = [rows_of(ref, chunk, size) for ref in (q_all, full_all, back_all)]

    @pl.when(step == 0)
    def _():
        tail[...] = jnp.zeros_like(tail)

    columns = spread_columns(zl_ref[...], zr_ref[...])
    masked = [columns * mask_ref[comp] for comp in range(3)]
    sub = rows_carry
    total = tail[...]
    for part in range(size // sub - 1, -1, -1):
        rows = slice(part * sub, (part + 1) * sub)
        flat = slice(part * sub * lines, (part + 1) * sub * lines)
        edge = jnp.concatenate([masked[comp][flat] for comp in range(3)], axis=0)
        full_ref[:, rows] = q_ref[:, rows] + dot(edge, pz_ref[...]).reshape(3, sub, lines, count)
        for i in range((part + 1) * sub - 1, part * sub - 1, -1):
            total = full_ref[:, i] + rate * total
            back_ref[:, i] = total
    tail[...] = total


def corner_body(xright_ref, xleft_ref, zl_ref, zr_ref, tr_ref, tl_ref, pz_ref, mask_ref, right_ref, left_ref):
    near = tr_ref.shape[0] // 3
    planes = jnp.concatenate([zl_ref[...], zr_ref[...]], axis=0)
    span = planes.shape[1]
    terms = right_ref.shape[0]
    lines = right_ref.shape[2]
    found = []
    for block, table in ((planes[:, span - near:], tr_ref), (planes[:, :near], tl_ref)):
        hi, lo = parts(block)
        found.append(dot(jnp.concatenate([hi, lo, hi], axis=1), table[...]))
    group = zl_ref.shape[0]
    both = jnp.concatenate(found, axis=1)
    columns = spread_columns(both[:group], both[group:])
    used = terms * lines
    columns = jnp.concatenate([columns[:used], columns[LANES:LANES + used]], axis=0)
    add = dot(jnp.concatenate([columns * mask_ref[comp] for comp in range(3)], axis=0), pz_ref[...])
    for comp in range(3):
        for term in range(terms):
            at = (2 * comp) * used + term * lines
            right_ref[term, comp] = xright_ref[term, comp] + add[at:at + lines]
            left_ref[term, comp] = xleft_ref[term, comp] + add[used + at:used + at + lines]


def filter_body(n_blocks, consts, q_all, back_all, xl_ref, xr_ref, out_ref, lead):
    step = pl.program_id(0)
    size = out_ref.shape[1]
    rate = consts["rate_f"]
    q_ref, back_ref = [rows_of(ref, step, size) for ref in (q_all, back_all)]
    last = step == n_blocks - 1
    following = rows_of(q_all, jnp.minimum(step + 1, n_blocks - 1), size)
    beyond = [jnp.where(last, xr_ref[1 + k], following[:, k]) for k in range(2)]

    @pl.when(step == 0)
    def _():
        lead[0] = (xl_ref[0] + rate * back_ref[:, 0]) * (1.0 / (1.0 - rate * rate))
        lead[1] = xl_ref[1]
        lead[2] = xl_ref[2]

    total, one, two = lead[0], lead[1], lead[2]
    here = q_ref[:, 0]
    ahead = q_ref[:, 1]
    for i in range(size):
        further = q_ref[:, i + 2] if i + 2 < size else beyond[i + 2 - size]
        total = back_ref[:, i] + rate * total
        out_ref[:, i] = (
            here
            + consts["s0"] * total
            + consts["s1"] * (ahead + one)
            + consts["s2"] * (further + two)
        )
        two = one
        one = here
        here = ahead
        ahead = further
    lead[0] = total
    lead[1] = one
    lead[2] = two
    for chunk_at in range((near_filter + size - 1) // size):
        offset = chunk_at * size

        @pl.when(step == n_blocks - 1 - chunk_at)
        def _():
            later = xr_ref[0]
            for k in range(min(size, near_filter - offset)):
                i = size - 1 - k
                weight = consts["s0"] * rate ** (offset + k + 1) / (1.0 - rate * rate)
                out_ref[:, i] = out_ref[:, i] + weight * later


def whole(shape):
    return pl.BlockSpec(shape, lambda t: (0,) * len(shape))


def in_hbm(values):
    return pltpu.with_memory_space_constraint(values, pltpu.HBM)


def ring(count, step):
    return [(i, (i + step) % count) for i in range(count)]


def swap(right, left, axis):
    count = lax.axis_size(axis)
    return (
        lax.ppermute(right, axis, ring(count, 1)),
        lax.ppermute(left, axis, ring(count, -1)),
    )


def shards(velocity, prior):
    comps, cells_x, lines, cells_z = velocity.shape
    spacing_x = 8.0 * math.pi / (cells_x * lax.axis_size("gx"))
    spacing_z = 3.0 * math.pi / (cells_z * lax.axis_size("gz"))
    dt_step = 0.3 / (1.0 / spacing_x + 1.0 / spacing_z)
    rate_d = decay_rate(alpha_deriv)
    rate_f = decay_rate(alpha_filter)
    size = rows_block
    n_blocks = cells_x // size
    span = cells_x * lines

    taps_x = deriv_taps(spacing_x)
    flat_part = taps_x[2] / alpha_deriv
    solve_part = (taps_x[1] - flat_part) * (-rate_d / alpha_deriv)
    kf = kernel_values([0, 1, 2, 3], filter_taps(), alpha_filter)
    half = filter_taps()
    t2 = half[3] / alpha_filter
    t1 = (half[2] - t2) / alpha_filter
    t0 = (half[1] - 3.0 * half[3] - t1) / alpha_filter
    rest = half[0] - 2.0 * half[2] - t0
    main = t0 + 2.0 * t2
    scale_f = 5.0 / 12.0 * main
    consts = {
        "rate_d": rate_d,
        "ratio_d": flat_part / solve_part,
        "x_factor": -dt_step * solve_part,
        "rate_f": rate_f,
        "s0": rest * (-rate_f / alpha_filter) / main,
        "s1": t1 / main,
        "s2": t2 / main,
        "e3": float(scale_f * kf[3] / rate_f**3),
        "e1": float(scale_f * (kf[1] - kf[3] / rate_f**2)),
        "e2": float(scale_f * (kf[2] - kf[3] / rate_f)),
    }

    plane = (comps, lines, cells_z)
    big = lambda rows, idx: pl.BlockSpec((comps, rows, lines, cells_z), lambda t: (0, idx(t), 0, 0))
    thin = lambda group, rows, idx: pl.BlockSpec((group, rows * lines), lambda t: (0, idx(t)))
    edge = (2,) + plane
    group_d = 8
    taps_z = deriv_taps(spacing_z)
    cell = np.arange(near_deriv)
    weights = np.stack(
        [-dt_step * kernel_values(cell - near_deriv - term, taps_z, alpha_deriv) for term in range(2)]
        + [-dt_step * kernel_values(cell + 1 + term, taps_z, alpha_deriv) for term in range(2)]
    )
    weights = jnp.asarray(np.broadcast_to(weights[:, :, None], (4, near_deriv, LANES)), f32)
    n_edge = cells_x // rows_edge
    held = pl.BlockSpec(memory_space=pltpu.VMEM)
    dz = jnp.asarray(band_matrix(cells_z, taps_z, alpha_deriv, -dt_step))
    zr_send, zl_send, xr_send, xl_send, field_in, dz = pl.pallas_call(
        functools.partial(edge_body, rate_d, n_edge),
        grid=(n_edge,),
        in_specs=[
            pl.BlockSpec(memory_space=pltpu.HBM), whole(weights.shape),
            pl.BlockSpec(memory_space=pltpu.HBM),
        ],
        out_specs=[thin(group_d, rows_edge, lambda t: t)] * 2 + [whole(edge)] * 2 + [held] * 2,
        out_shape=[jax.ShapeDtypeStruct((group_d, span), f32)] * 2
        + [jax.ShapeDtypeStruct(edge, f32)] * 2
        + [jax.ShapeDtypeStruct(velocity.shape, f32), jax.ShapeDtypeStruct(dz.shape, bf16)],
        scratch_shapes=[pltpu.SemaphoreType.DMA((n_edge + 1,))],
        name="edges",
        compiler_params=pltpu.CompilerParams(vmem_limit_bytes=limits["edges"] << 20),
    )(in_hbm(velocity), in_hbm(weights), in_hbm(dz))
    xl, xr = swap(xr_send, xl_send, "gx")
    zl, zr = swap(zr_send, zl_send, "gz")

    group_f = 16
    plain = lambda t: t
    edge3 = (3,) + plane
    block = (comps, size, lines, cells_z)
    field = jax.ShapeDtypeStruct(velocity.shape, f32)
    heads_shape = (n_blocks, 2) + plane
    slope, back, base, heads = pl.pallas_call(
        functools.partial(local_body, n_blocks, consts),
        grid=(n_blocks,),
        in_specs=[held, held, held],
        out_specs=[held, held, held, whole(heads_shape)],
        out_shape=[field] * 3 + [jax.ShapeDtypeStruct(heads_shape, f32)],
        scratch_shapes=[pltpu.VMEM(plane, f32)],
        name="local",
        compiler_params=pltpu.CompilerParams(vmem_limit_bytes=limits["local"] << 20),
        cost_estimate=pl.CostEstimate(flops=2 * 6144 * 768 * 256, bytes_accessed=25 << 20, transcendentals=0),
    )(field_in, prior, dz)

    pd = jnp.asarray(padded_profiles(edge_profiles(cells_z, alpha_deriv, 2, group_d)))
    mask_d = component_masks(2, group_d)
    decay = np.power(rate_f, np.arange(near_filter))
    decay = np.stack([decay[::-1], decay])
    decay = jnp.asarray(np.broadcast_to(decay[:, :, None], (2, near_filter, LANES)), f32)
    advance, prov, zr_send, zl_send = pl.pallas_call(
        functools.partial(advance_body, n_blocks, consts),
        grid=(n_blocks,),
        in_specs=[held, held, held, held] + [
            whole(heads_shape), whole(edge), whole(edge),
            thin(group_d, size, plain), thin(group_d, size, plain),
            whole(pd.shape), whole(mask_d.shape), whole(decay.shape),
        ],
        out_specs=[big(size, plain), held] + [thin(group_f, size, plain)] * 2,
        out_shape=[field] * 2 + [jax.ShapeDtypeStruct((group_f, span), f32)] * 2,
        scratch_shapes=[pltpu.VMEM(block, f32), pltpu.VMEM((3,) + plane, f32)],
        name="advance",
        compiler_params=pltpu.CompilerParams(vmem_limit_bytes=limits["advance"] << 20),
    )(field_in, slope, back, base, heads, xl, xr, zl, zr, pd, mask_d, decay)
    zl, zr = swap(zr_send, zl_send, "gz")

    fz = jnp.asarray(band_matrix(cells_z, filter_taps(), alpha_filter, scale_f))
    pf = jnp.asarray(padded_profiles(edge_profiles(cells_z, alpha_filter, 3, group_f)))
    mask_f = component_masks(3, group_f)
    q, xr_part, xl_part = pl.pallas_call(
        functools.partial(smooth_body, n_blocks, consts),
        grid=(n_blocks,),
        in_specs=[held, whole(fz.shape)],
        out_specs=[held, whole(edge3), whole(edge3)],
        out_shape=[field] + [jax.ShapeDtypeStruct(edge3, f32)] * 2,
        scratch_shapes=[pltpu.VMEM((2,) + plane, f32)],
        name="smooth",
        compiler_params=pltpu.CompilerParams(vmem_limit_bytes=limits["smooth"] << 20),
        cost_estimate=pl.CostEstimate(flops=2 * 6144 * 768 * 256, bytes_accessed=12 << 20, transcendentals=0),
    )(prov, fz)

    near = near_filter * lines
    cell = np.arange(cells_x)[:, None, None, None]
    line = (np.arange(lines)[None, :, None, None] == np.arange(lines)[None, None, None, :]) * 1.0
    grow = np.power(rate_f, cells_x - 1 - cell)
    pick = np.concatenate([grow, cell == cells_x - 1, cell == cells_x - 2], axis=2) * 1.0
    right_table = (pick * line).reshape(span, 3 * lines)
    left_table = (pick[::-1] * line).reshape(span, 3 * lines)
    widen = lambda t: np.concatenate([t, np.zeros((near, 128 - t.shape[1]))], axis=1)
    triple = lambda t: jnp.asarray(np.concatenate([np_parts(t)[k] for k in (0, 0, 1)], axis=0))
    tr = triple(widen(right_table[span - near:]))
    tl = triple(widen(left_table[:near]))
    xr_send, xl_send = pl.pallas_call(
        corner_body,
        grid=(1,),
        in_specs=[
            whole(edge3), whole(edge3), whole((group_f, span)), whole((group_f, span)),
            whole(tr.shape), whole(tl.shape), whole(pf.shape), whole(mask_f.shape),
        ],
        out_specs=[whole(edge3)] * 2,
        out_shape=[jax.ShapeDtypeStruct(edge3, f32)] * 2,
        name="corner",
        compiler_params=pltpu.CompilerParams(vmem_limit_bytes=8 << 20),
    )(xr_part, xl_part, zl, zr, tr, tl, pf, mask_f)
    xl, xr = swap(xr_send, xl_send, "gx")

    n_parts = cells_x // rows_filter
    backward = lambda t: n_parts - 1 - t
    q, back = pl.pallas_call(
        functools.partial(carry_body, n_parts, rate_f),
        grid=(n_parts,),
        in_specs=[
            held, thin(group_f, rows_filter, backward), thin(group_f, rows_filter, backward),
            whole(pf.shape), whole(mask_f.shape),
        ],
        out_specs=[held, held],
        out_shape=[field, field],
        scratch_shapes=[pltpu.VMEM(plane, f32)],
        name="carry",
        compiler_params=pltpu.CompilerParams(vmem_limit_bytes=limits["carry"] << 20),
        cost_estimate=pl.CostEstimate(flops=2 * 6144 * 128 * 256, bytes_accessed=12 << 20, transcendentals=0),
    )(q, zl, zr, pf, mask_f)
    filtered = pl.pallas_call(
        functools.partial(filter_body, n_parts, consts),
        grid=(n_parts,),
        in_specs=[held, held, whole(edge3), whole(edge3)],
        out_specs=big(rows_filter, plain),
        out_shape=field,
        scratch_shapes=[pltpu.VMEM((3,) + plane, f32)],
        name="filter",
        compiler_params=pltpu.CompilerParams(vmem_limit_bytes=limits["filter"] << 20),
    )(q, back, xl, xr)
    return (filtered, advance)


def solution(mesh):
    placed = P(None, "gx", None, "gz")
    return jax.shard_map(
        shards,
        mesh=mesh,
        in_specs=(placed, placed),
        out_specs=(placed, placed),
        check_vma=False,
    )
```

```python
import functools
import math

import jax
import jax.numpy as jnp
import numpy as np
from jax import lax
from jax.experimental import pallas as pl
from jax.experimental.pallas import tpu as pltpu
from jax.sharding import PartitionSpec as P

alpha_deriv = 1.0 / 3.0
alpha_filter = 0.49
rows_edge = 64
rows_block = 64
rows_sub = 64
rows_local = 8
rows_smooth = 16
rows_carry = 16
limits = {"edges": 6, "local": 8, "advance": 10, "smooth": 6, "carry": 5, "filter": 8}
rows_filter = 64
near_deriv = 32
near_filter = 96
LANES = 128
bf16 = jnp.bfloat16
f32 = jnp.float32


def decay_rate(alpha):
    return (-1.0 + math.sqrt(1.0 - 4.0 * alpha * alpha)) / (2.0 * alpha)


def green_scale(alpha):
    return 1.0 / (1.0 + 2.0 * alpha * decay_rate(alpha))


def kernel_values(offsets, taps, alpha):
    offsets = np.asarray(offsets, dtype=np.float64)
    total = np.zeros_like(offsets)
    for shift, weight in taps.items():
        total = total + weight * green_scale(alpha) * np.power(
            decay_rate(alpha), np.abs(offsets - shift)
        )
    return total


def deriv_taps(spacing):
    near = 14.0 / 9.0 / (2.0 * spacing)
    far = 1.0 / 9.0 / (4.0 * spacing)
    return {1: near, -1: -near, 2: far, -2: -far}


def filter_taps():
    taps = {0: (11.0 + 10.0 * alpha_filter) / 16.0}
    weights = (
        (15.0 + 34.0 * alpha_filter) / 32.0,
        (-3.0 + 6.0 * alpha_filter) / 16.0,
        (1.0 - 2.0 * alpha_filter) / 32.0,
    )
    for shift, weight in enumerate(weights, 1):
        taps[shift] = 0.5 * weight
        taps[-shift] = 0.5 * weight
    return taps


def parts(values):
    high = values.astype(bf16)
    low = (values - high.astype(f32)).astype(bf16)
    return high, low


def np_parts(values):
    values = np.asarray(values, dtype=np.float32)
    high = values.astype(bf16)
    low = (values - high.astype(np.float32)).astype(bf16)
    return high, low


def band_matrix(count, taps, alpha, factor):
    source = np.arange(count)[:, None]
    target = np.arange(count)[None, :]
    high, low = np_parts(factor * kernel_values(source - target, taps, alpha))
    return np.concatenate([high, high, low], axis=0)


def edge_profiles(count, alpha, terms, group):
    cell = np.arange(count)
    table = np.zeros((2 * group, count))
    rate = decay_rate(alpha)
    for term in range(terms):
        if term < terms - 1:
            shape = (cell == term) * 1.0
        else:
            shape = np.where(cell >= term, np.power(rate, np.maximum(cell - term, 0)), 0.0)
        for comp in range(3):
            table[term * 3 + comp] = shape
            table[group + term * 3 + comp] = shape[::-1]
    return table


def padded_profiles(table):
    high, low = np_parts(table)
    rest = np.zeros((LANES - 3 * table.shape[0], table.shape[1]), dtype=bf16)
    return np.concatenate([high, high, low, rest], axis=0)


def component_masks(terms, group):
    lane = np.arange(LANES)
    row = lane % group
    masks = [(lane < 6 * group) & (row < 3 * terms) & (row % 3 == comp) for comp in range(3)]
    return jnp.asarray(np.stack(masks)[:, None, :], bf16)


def spread_columns(left, right):
    both = jnp.concatenate([left, right], axis=0)
    high = both.astype(bf16).astype(f32)
    low = both - high
    rest = jnp.zeros((128 - 3 * both.shape[0], both.shape[1]), f32)
    return jnp.concatenate([high, low, high, rest], axis=0).T.astype(bf16)


def dot(a, b):
    return jnp.dot(a, b, preferred_element_type=f32)


def rows_of(ref, chunk, size):
    return ref.at[:, pl.ds(chunk * size, size)]


def edge_body(
    rate, n_blocks,
    v_hbm, weight_ref, table_hbm,
    zright_ref, zleft_ref, xright_ref, xleft_ref, v_all, table_ref,
    sems,
):
    step = pl.program_id(0)
    cells, lines, count = v_all.shape[1:]
    size = cells // n_blocks

    def fetch(chunk):
        rows = pl.ds(chunk * size, size)
        return pltpu.make_async_copy(v_hbm.at[:, rows], v_all.at[:, rows], sems.at[chunk])

    table = pltpu.make_async_copy(table_hbm, table_ref, sems.at[n_blocks])

    @pl.when(step == 0)
    def _():
        for chunk in range(n_blocks):
            fetch(chunk).start()
        table.start()

    fetch(step).wait()
    v_ref = rows_of(v_all, step, size)
    near = weight_ref.shape[1]
    group = LANES // lines
    left_lane = lax.broadcasted_iota(jnp.int32, (LANES, LANES), 1) < LANES // 2
    for comp in range(3):
        for part in range(size // group):
            block = v_ref[comp, part * group:(part + 1) * group].reshape(LANES, count)
            both = jnp.where(left_lane, block[:, :LANES], block[:, count - LANES:]).T
            span = slice(part * LANES, (part + 1) * LANES)
            for term in range(2):
                row = term * 3 + comp
                zright_ref[row:row + 1, span] = jnp.sum(
                    both[LANES - near:] * weight_ref[term], axis=0, keepdims=True
                )
                zleft_ref[row:row + 1, span] = jnp.sum(
                    both[:near] * weight_ref[2 + term], axis=0, keepdims=True
                )
    for row in range(6, 8):
        zright_ref[row:row + 1, :] = jnp.zeros((1, size * lines), f32)
        zleft_ref[row:row + 1, :] = jnp.zeros((1, size * lines), f32)

    @pl.when(step == 0)
    def _():
        total = v_ref[:, near_deriv - 1]
        for i in range(near_deriv - 2, -1, -1):
            total = rate * total + v_ref[:, i]
        xleft_ref[0] = total
        xleft_ref[1] = v_ref[:, 0]

    @pl.when(step == pl.num_programs(0) - 1)
    def _():
        total = v_ref[:, size - near_deriv]
        for i in range(size - near_deriv + 1, size):
            total = rate * total + v_ref[:, i]
        xright_ref[0] = total
        xright_ref[1] = v_ref[:, size - 1]
        table.wait()


def weighted_rows(ref, weights):
    sums = [None] * 4
    for k, (row, weight) in enumerate(weights):
        term = weight * ref[:, row]
        sums[k % 4] = term if sums[k % 4] is None else sums[k % 4] + term
    return (sums[0] + sums[1]) + (sums[2] + sums[3])


def local_body(
    n_blocks, consts, v_all, prior_all, dz_ref, slope_all, back_all, base_all, heads_ref, tail
):
    step = pl.program_id(0)
    cells, lines, count = v_all.shape[1:]
    size = cells // n_blocks
    rate = consts["rate_d"]
    chunk = n_blocks - 1 - step
    v_ref, prior_ref, slope_ref, back_ref, base_ref = [
        rows_of(ref, chunk, size) for ref in (v_all, prior_all, slope_all, back_all, base_all)
    ]

    @pl.when(step == 0)
    def _():
        tail[...] = jnp.zeros_like(tail)

    sub = rows_local
    total = tail[...]
    for part in range(size // sub - 1, -1, -1):
        rows = slice(part * sub, (part + 1) * sub)
        hi, lo = parts(v_ref[:, rows].reshape(3 * sub * lines, count))
        lhs = jnp.concatenate([hi, lo, hi], axis=1)
        slope_ref[:, rows] = dot(lhs, dz_ref[...]).reshape(3, sub, lines, count)
        for i in range((part + 1) * sub - 1, part * sub - 1, -1):
            here = v_ref[:, i]
            total = here + rate * total
            back_ref[:, i] = total
            base_ref[:, i] = 2.4 * here - 0.68 * prior_ref[:, i]
    tail[...] = total
    heads_ref[chunk, 0] = total
    heads_ref[chunk, 1] = v_ref[:, 0]


def advance_body(
    n_blocks, consts,
    v_all, slope_all, back_all, base_all, heads_ref, xl_ref, xr_ref, zl_ref, zr_ref,
    pz_ref, mask_ref, weight_ref,
    adv_ref, prov_all, zright_ref, zleft_ref,
    extra, lead,
):
    step = pl.program_id(0)
    size, lines, count = adv_ref.shape[1:]
    v_ref, slope_ref, back_ref, base_ref, prov_ref = [
        rows_of(ref, step, size) for ref in (v_all, slope_all, back_all, base_all, prov_all)
    ]
    sub = rows_sub
    rate = consts["rate_d"]
    ratio = consts["ratio_d"]
    near = weight_ref.shape[1]

    @pl.when(step == 0)
    def _():
        before = (xl_ref[0] + rate * back_ref[:, 0]) * (1.0 / (1.0 - rate * rate))
        value = back_ref[:, 0] + rate * before
        lead[0] = value
        lead[1] = before + ratio * xl_ref[1]
        lead[2] = value + ratio * v_ref[:, 0]

    columns = spread_columns(zl_ref[...], zr_ref[...])
    edge = jnp.concatenate([columns * mask_ref[comp] for comp in range(3)], axis=0)
    extra[...] = dot(edge, pz_ref[...]).reshape(3, size, lines, count)
    last = step == n_blocks - 1
    following = jnp.minimum(step + 1, n_blocks - 1)
    beyond = jnp.where(last, xr_ref[0], 0.0)
    back_next = jnp.where(last, xr_ref[0], heads_ref[following, 0])
    here_next = jnp.where(last, xr_ref[1], heads_ref[following, 1])
    value, behind, level = lead[0], lead[1], lead[2]
    here = v_ref[:, 0]
    for part in range(size // sub):
        for i in range(part * sub, (part + 1) * sub):
            if i + 1 < size:
                ahead = v_ref[:, i + 1]
                back = back_ref[:, i + 1]
                if size - 1 - i <= near_deriv:
                    back = back + (rate ** (size - 1 - i)) * beyond
            else:
                ahead = here_next
                back = back_next
            value = back + rate * value
            above = value + ratio * ahead
            gx = above - behind
            behind = level
            level = above
            ux = consts["x_factor"] * here[0]
            adv = ux[None] * gx + here[2][None] * (slope_ref[:, i] + extra[:, i])
            adv_ref[:, i] = adv
            prov_ref[:, i] = base_ref[:, i] + adv
            here = ahead
        for comp in range(3):
            for piece in range(sub * lines // LANES):
                first = part * sub + piece * (LANES // lines)
                tile = prov_ref[comp, first:first + LANES // lines].reshape(LANES, count)
                lanes = slice(first * lines, first * lines + LANES)
                right = tile[:, count - LANES:].T
                left = tile[:, :LANES].T
                for ref, near_part, f0, f1, weight in (
                    (zright_ref, right[LANES - near:], right[127:128], right[126:127], weight_ref[0]),
                    (zleft_ref, left[:near], left[0:1], left[1:2], weight_ref[1]),
                ):
                    cs = consts["e3"] * jnp.sum(near_part * weight, axis=0, keepdims=True)
                    r = consts["rate_f"]
                    ref[comp:comp + 1, lanes] = r * cs + consts["e1"] * f0 + consts["e2"] * f1
                    ref[3 + comp:4 + comp, lanes] = (r * r) * cs + consts["e2"] * f0
                    ref[6 + comp:7 + comp, lanes] = (r * r * r) * cs
    lead[0] = value
    lead[1] = behind
    lead[2] = level
    for ref in (zright_ref, zleft_ref):
        ref[9:16, :] = jnp.zeros((7, size * lines), f32)


def smooth_body(n_blocks, consts, prov_all, fz_ref, q_all, xright_ref, xleft_ref, qsum):
    step = pl.program_id(0)
    cells, lines, count = prov_all.shape[1:]
    size = cells // n_blocks
    prov_ref, q_ref = [rows_of(ref, step, size) for ref in (prov_all, q_all)]
    rate = consts["rate_f"]

    @pl.when(step == 0)
    def _():
        qsum[...] = jnp.zeros_like(qsum)

    sub = rows_smooth
    for part in range(size // sub):
        rows = slice(part * sub, (part + 1) * sub)
        hi, lo = parts(prov_ref[:, rows].reshape(3 * sub * lines, count))
        lhs = jnp.concatenate([hi, lo, hi], axis=1)
        q_ref[:, rows] = dot(lhs, fz_ref[...]).reshape(3, sub, lines, count)
    for chunk_at in range((near_filter + size - 1) // size):
        offset = chunk_at * size
        used = min(size, near_filter - offset)

        @pl.when(step == chunk_at)
        def _():
            spots = [(i, rate ** (offset + i)) for i in range(used)]
            qsum[0] = qsum[0] + weighted_rows(q_ref, spots)

        @pl.when(step == n_blocks - 1 - chunk_at)
        def _():
            spots = [(size - 1 - i, rate ** (offset + i)) for i in range(used)]
            qsum[1] = qsum[1] + weighted_rows(q_ref, spots)

    @pl.when(step == 0)
    def _():
        xleft_ref[1] = q_ref[:, 0]
        xleft_ref[2] = q_ref[:, 1]

    @pl.when(step == n_blocks - 1)
    def _():
        xleft_ref[0] = qsum[0]
        xright_ref[0] = qsum[1]
        xright_ref[1] = q_ref[:, size - 1]
        xright_ref[2] = q_ref[:, size - 2]


def carry_body(n_blocks, rate, q_all, zl_ref, zr_ref, pz_ref, mask_ref, full_all, back_all, tail):
    step = pl.program_id(0)
    cells, lines, count = q_all.shape[1:]
    size = cells // n_blocks
    chunk = n_blocks - 1 - step
    q_ref, full_ref, back_ref = [rows_of(ref, chunk, size) for ref in (q_all, full_all, back_all)]

    @pl.when(step == 0)
    def _():
        tail[...] = jnp.zeros_like(tail)

    columns = spread_columns(zl_ref[...], zr_ref[...])
    masked = [columns * mask_ref[comp] for comp in range(3)]
    sub = rows_carry
    total = tail[...]
    for part in range(size // sub - 1, -1, -1):
        rows = slice(part * sub, (part + 1) * sub)
        flat = slice(part * sub * lines, (part + 1) * sub * lines)
        edge = jnp.concatenate([masked[comp][flat] for comp in range(3)], axis=0)
        full_ref[:, rows] = q_ref[:, rows] + dot(edge, pz_ref[...]).reshape(3, sub, lines, count)
        for i in range((part + 1) * sub - 1, part * sub - 1, -1):
            total = full_ref[:, i] + rate * total
            back_ref[:, i] = total
    tail[...] = total


def corner_body(xright_ref, xleft_ref, zl_ref, zr_ref, tr_ref, tl_ref, pz_ref, mask_ref, right_ref, left_ref):
    near = tr_ref.shape[0] // 3
    planes = jnp.concatenate([zl_ref[...], zr_ref[...]], axis=0)
    span = planes.shape[1]
    terms = right_ref.shape[0]
    lines = right_ref.shape[2]
    found = []
    for block, table in ((planes[:, span - near:], tr_ref), (planes[:, :near], tl_ref)):
        hi, lo = parts(block)
        found.append(dot(jnp.concatenate([hi, lo, hi], axis=1), table[...]))
    group = zl_ref.shape[0]
    both = jnp.concatenate(found, axis=1)
    columns = spread_columns(both[:group], both[group:])
    used = terms * lines
    columns = jnp.concatenate([columns[:used], columns[LANES:LANES + used]], axis=0)
    add = dot(jnp.concatenate([columns * mask_ref[comp] for comp in range(3)], axis=0), pz_ref[...])
    for comp in range(3):
        for term in range(terms):
            at = (2 * comp) * used + term * lines
            right_ref[term, comp] = xright_ref[term, comp] + add[at:at + lines]
            left_ref[term, comp] = xleft_ref[term, comp] + add[used + at:used + at + lines]


def filter_rows(consts, q_ref, back_ref, out_ref, state, beyond):
    size = q_ref.shape[1]
    total, one, two = state
    here = q_ref[:, 0]
    ahead = q_ref[:, 1]
    for i in range(size):
        further = q_ref[:, i + 2] if i + 2 < size else beyond[i + 2 - size]
        total = back_ref[:, i] + consts["rate_f"] * total
        out_ref[:, i] = (
            here
            + consts["s0"] * total
            + consts["s1"] * (ahead + one)
            + consts["s2"] * (further + two)
        )
        two = one
        one = here
        here = ahead
        ahead = further
    return total, one, two


def middle_body(n_blocks, consts, q_all, back_all, mid_all, last_ref, lead):
    step = pl.program_id(0)
    size = q_all.shape[1] // n_blocks
    q_ref, back_ref = [rows_of(ref, step, size) for ref in (q_all, back_all)]

    @pl.when(step == 0)
    def _():
        total = back_ref[:, 0]
        for i in range(1, size):
            total = back_ref[:, i] + consts["rate_f"] * total
        lead[0] = total
        lead[1] = q_ref[:, size - 1]
        lead[2] = q_ref[:, size - 2]

    @pl.when(step > 0)
    def _():
        following = rows_of(q_all, step + 1, size)
        state = filter_rows(
            consts, q_ref, back_ref, rows_of(mid_all, step - 1, size),
            (lead[0], lead[1], lead[2]), (following[:, 0], following[:, 1]),
        )
        for k in range(3):
            lead[k] = state[k]

    @pl.when(step == n_blocks - 2)
    def _():
        last_ref[...] = lead[0]


def filter_body(
    n_blocks, consts, q_all, back_all, mid_all, last_ref, xl_ref, xr_ref, out_ref, lead, before
):
    step = pl.program_id(0)
    size = out_ref.shape[1]
    rate = consts["rate_f"]
    q_ref, back_ref = [rows_of(ref, step, size) for ref in (q_all, back_all)]
    last = step == n_blocks - 1
    inner = jnp.logical_and(step > 0, step < n_blocks - 1)

    @pl.when(step == 0)
    def _():
        before[...] = (xl_ref[0] + rate * back_ref[:, 0]) * (1.0 / (1.0 - rate * rate))
        lead[0] = before[...]
        lead[1] = xl_ref[1]
        lead[2] = xl_ref[2]

    @pl.when(last)
    def _():
        prior_rows = rows_of(q_all, step - 1, size)
        lead[0] = last_ref[...]
        lead[1] = prior_rows[:, size - 1]
        lead[2] = prior_rows[:, size - 2]

    @pl.when(jnp.logical_not(inner))
    def _():
        following = rows_of(q_all, jnp.minimum(step + 1, n_blocks - 1), size)
        beyond = [jnp.where(last, xr_ref[1 + k], following[:, k]) for k in range(2)]
        filter_rows(consts, q_ref, back_ref, out_ref, (lead[0], lead[1], lead[2]), beyond)

    @pl.when(inner)
    def _():
        out_ref[...] = rows_of(mid_all, step - 1, size)[...]

    for chunk_at in range((near_filter + size - 1) // size):
        offset = chunk_at * size
        used = min(size, near_filter - offset)
        if chunk_at > 0:

            @pl.when(step == chunk_at)
            def _():
                earlier = before[...]
                for i in range(used):
                    weight = consts["s0"] * rate ** (offset + i + 1)
                    out_ref[:, i] = out_ref[:, i] + weight * earlier

        @pl.when(step == n_blocks - 1 - chunk_at)
        def _():
            later = xr_ref[0]
            for k in range(used):
                i = size - 1 - k
                weight = consts["s0"] * rate ** (offset + k + 1) / (1.0 - rate * rate)
                out_ref[:, i] = out_ref[:, i] + weight * later


def whole(shape):
    return pl.BlockSpec(shape, lambda t: (0,) * len(shape))


def in_hbm(values):
    return pltpu.with_memory_space_constraint(values, pltpu.HBM)


def ring(count, step):
    return [(i, (i + step) % count) for i in range(count)]


def swap(right, left, axis):
    count = lax.axis_size(axis)
    return (
        lax.ppermute(right, axis, ring(count, 1)),
        lax.ppermute(left, axis, ring(count, -1)),
    )


def shards(velocity, prior):
    comps, cells_x, lines, cells_z = velocity.shape
    spacing_x = 8.0 * math.pi / (cells_x * lax.axis_size("gx"))
    spacing_z = 3.0 * math.pi / (cells_z * lax.axis_size("gz"))
    dt_step = 0.3 / (1.0 / spacing_x + 1.0 / spacing_z)
    rate_d = decay_rate(alpha_deriv)
    rate_f = decay_rate(alpha_filter)
    size = rows_block
    n_blocks = cells_x // size
    span = cells_x * lines

    taps_x = deriv_taps(spacing_x)
    flat_part = taps_x[2] / alpha_deriv
    solve_part = (taps_x[1] - flat_part) * (-rate_d / alpha_deriv)
    kf = kernel_values([0, 1, 2, 3], filter_taps(), alpha_filter)
    half = filter_taps()
    t2 = half[3] / alpha_filter
    t1 = (half[2] - t2) / alpha_filter
    t0 = (half[1] - 3.0 * half[3] - t1) / alpha_filter
    rest = half[0] - 2.0 * half[2] - t0
    main = t0 + 2.0 * t2
    scale_f = 5.0 / 12.0 * main
    consts = {
        "rate_d": rate_d,
        "ratio_d": flat_part / solve_part,
        "x_factor": -dt_step * solve_part,
        "rate_f": rate_f,
        "s0": rest * (-rate_f / alpha_filter) / main,
        "s1": t1 / main,
        "s2": t2 / main,
        "e3": float(scale_f * kf[3] / rate_f**3),
        "e1": float(scale_f * (kf[1] - kf[3] / rate_f**2)),
        "e2": float(scale_f * (kf[2] - kf[3] / rate_f)),
    }

    plane = (comps, lines, cells_z)
    big = lambda rows, idx: pl.BlockSpec((comps, rows, lines, cells_z), lambda t: (0, idx(t), 0, 0))
    thin = lambda group, rows, idx: pl.BlockSpec((group, rows * lines), lambda t: (0, idx(t)))
    edge = (2,) + plane
    group_d = 8
    taps_z = deriv_taps(spacing_z)
    cell = np.arange(near_deriv)
    weights = np.stack(
        [-dt_step * kernel_values(cell - near_deriv - term, taps_z, alpha_deriv) for term in range(2)]
        + [-dt_step * kernel_values(cell + 1 + term, taps_z, alpha_deriv) for term in range(2)]
    )
    weights = jnp.asarray(np.broadcast_to(weights[:, :, None], (4, near_deriv, LANES)), f32)
    n_edge = cells_x // rows_edge
    held = pl.BlockSpec(memory_space=pltpu.VMEM)
    dz = jnp.asarray(band_matrix(cells_z, taps_z, alpha_deriv, -dt_step))
    zr_send, zl_send, xr_send, xl_send, field_in, dz = pl.pallas_call(
        functools.partial(edge_body, rate_d, n_edge),
        grid=(n_edge,),
        in_specs=[
            pl.BlockSpec(memory_space=pltpu.HBM), whole(weights.shape),
            pl.BlockSpec(memory_space=pltpu.HBM),
        ],
        out_specs=[thin(group_d, rows_edge, lambda t: t)] * 2 + [whole(edge)] * 2 + [held] * 2,
        out_shape=[jax.ShapeDtypeStruct((group_d, span), f32)] * 2
        + [jax.ShapeDtypeStruct(edge, f32)] * 2
        + [jax.ShapeDtypeStruct(velocity.shape, f32), jax.ShapeDtypeStruct(dz.shape, bf16)],
        scratch_shapes=[pltpu.SemaphoreType.DMA((n_edge + 1,))],
        name="edges",
        compiler_params=pltpu.CompilerParams(vmem_limit_bytes=limits["edges"] << 20),
    )(in_hbm(velocity), in_hbm(weights), in_hbm(dz))
    xl, xr = swap(xr_send, xl_send, "gx")
    zl, zr = swap(zr_send, zl_send, "gz")

    group_f = 16
    plain = lambda t: t
    edge3 = (3,) + plane
    block = (comps, size, lines, cells_z)
    field = jax.ShapeDtypeStruct(velocity.shape, f32)
    heads_shape = (n_blocks, 2) + plane
    slope, back, base, heads = pl.pallas_call(
        functools.partial(local_body, n_blocks, consts),
        grid=(n_blocks,),
        in_specs=[held, held, held],
        out_specs=[held, held, held, whole(heads_shape)],
        out_shape=[field] * 3 + [jax.ShapeDtypeStruct(heads_shape, f32)],
        scratch_shapes=[pltpu.VMEM(plane, f32)],
        name="local",
        compiler_params=pltpu.CompilerParams(vmem_limit_bytes=limits["local"] << 20),
        cost_estimate=pl.CostEstimate(flops=2 * 6144 * 768 * 256, bytes_accessed=25 << 20, transcendentals=0),
    )(field_in, prior, dz)

    pd = jnp.asarray(padded_profiles(edge_profiles(cells_z, alpha_deriv, 2, group_d)))
    mask_d = component_masks(2, group_d)
    decay = np.power(rate_f, np.arange(near_filter))
    decay = np.stack([decay[::-1], decay])
    decay = jnp.asarray(np.broadcast_to(decay[:, :, None], (2, near_filter, LANES)), f32)
    advance, prov, zr_send, zl_send = pl.pallas_call(
        functools.partial(advance_body, n_blocks, consts),
        grid=(n_blocks,),
        in_specs=[held, held, held, held] + [
            whole(heads_shape), whole(edge), whole(edge),
            thin(group_d, size, plain), thin(group_d, size, plain),
            whole(pd.shape), whole(mask_d.shape), whole(decay.shape),
        ],
        out_specs=[big(size, plain), held] + [thin(group_f, size, plain)] * 2,
        out_shape=[field] * 2 + [jax.ShapeDtypeStruct((group_f, span), f32)] * 2,
        scratch_shapes=[pltpu.VMEM(block, f32), pltpu.VMEM((3,) + plane, f32)],
        name="advance",
        compiler_params=pltpu.CompilerParams(vmem_limit_bytes=limits["advance"] << 20),
    )(field_in, slope, back, base, heads, xl, xr, zl, zr, pd, mask_d, decay)
    zl, zr = swap(zr_send, zl_send, "gz")

    fz = jnp.asarray(band_matrix(cells_z, filter_taps(), alpha_filter, scale_f))
    pf = jnp.asarray(padded_profiles(edge_profiles(cells_z, alpha_filter, 3, group_f)))
    mask_f = component_masks(3, group_f)
    q, xr_part, xl_part = pl.pallas_call(
        functools.partial(smooth_body, n_blocks, consts),
        grid=(n_blocks,),
        in_specs=[held, whole(fz.shape)],
        out_specs=[held, whole(edge3), whole(edge3)],
        out_shape=[field] + [jax.ShapeDtypeStruct(edge3, f32)] * 2,
        scratch_shapes=[pltpu.VMEM((2,) + plane, f32)],
        name="smooth",
        compiler_params=pltpu.CompilerParams(vmem_limit_bytes=limits["smooth"] << 20),
        cost_estimate=pl.CostEstimate(flops=2 * 6144 * 768 * 256, bytes_accessed=12 << 20, transcendentals=0),
    )(prov, fz)

    near = near_filter * lines
    cell = np.arange(cells_x)[:, None, None, None]
    line = (np.arange(lines)[None, :, None, None] == np.arange(lines)[None, None, None, :]) * 1.0
    grow = np.power(rate_f, cells_x - 1 - cell)
    pick = np.concatenate([grow, cell == cells_x - 1, cell == cells_x - 2], axis=2) * 1.0
    right_table = (pick * line).reshape(span, 3 * lines)
    left_table = (pick[::-1] * line).reshape(span, 3 * lines)
    widen = lambda t: np.concatenate([t, np.zeros((near, 128 - t.shape[1]))], axis=1)
    triple = lambda t: jnp.asarray(np.concatenate([np_parts(t)[k] for k in (0, 0, 1)], axis=0))
    tr = triple(widen(right_table[span - near:]))
    tl = triple(widen(left_table[:near]))
    xr_send, xl_send = pl.pallas_call(
        corner_body,
        grid=(1,),
        in_specs=[
            whole(edge3), whole(edge3), whole((group_f, span)), whole((group_f, span)),
            whole(tr.shape), whole(tl.shape), whole(pf.shape), whole(mask_f.shape),
        ],
        out_specs=[whole(edge3)] * 2,
        out_shape=[jax.ShapeDtypeStruct(edge3, f32)] * 2,
        name="corner",
        compiler_params=pltpu.CompilerParams(vmem_limit_bytes=8 << 20),
    )(xr_part, xl_part, zl, zr, tr, tl, pf, mask_f)
    xl, xr = swap(xr_send, xl_send, "gx")

    n_parts = cells_x // rows_filter
    backward = lambda t: n_parts - 1 - t
    q, back = pl.pallas_call(
        functools.partial(carry_body, n_parts, rate_f),
        grid=(n_parts,),
        in_specs=[
            held, thin(group_f, rows_filter, backward), thin(group_f, rows_filter, backward),
            whole(pf.shape), whole(mask_f.shape),
        ],
        out_specs=[held, held],
        out_shape=[field, field],
        scratch_shapes=[pltpu.VMEM(plane, f32)],
        name="carry",
        compiler_params=pltpu.CompilerParams(vmem_limit_bytes=limits["carry"] << 20),
        cost_estimate=pl.CostEstimate(flops=2 * 6144 * 128 * 256, bytes_accessed=12 << 20, transcendentals=0),
    )(q, zl, zr, pf, mask_f)
    inside = (comps, (n_parts - 2) * rows_filter, lines, cells_z)
    mid, last = pl.pallas_call(
        functools.partial(middle_body, n_parts, consts),
        grid=(n_parts - 1,),
        in_specs=[held, held],
        out_specs=[held, held],
        out_shape=[jax.ShapeDtypeStruct(inside, f32), jax.ShapeDtypeStruct(plane, f32)],
        scratch_shapes=[pltpu.VMEM((3,) + plane, f32)],
        name="middle",
        compiler_params=pltpu.CompilerParams(vmem_limit_bytes=limits["carry"] << 20),
        cost_estimate=pl.CostEstimate(flops=20 << 20, bytes_accessed=12 << 20, transcendentals=0),
    )(q, back)
    filtered = pl.pallas_call(
        functools.partial(filter_body, n_parts, consts),
        grid=(n_parts,),
        in_specs=[held, held, held, held, whole(edge3), whole(edge3)],
        out_specs=big(rows_filter, plain),
        out_shape=field,
        scratch_shapes=[pltpu.VMEM((3,) + plane, f32), pltpu.VMEM(plane, f32)],
        name="filter",
        compiler_params=pltpu.CompilerParams(vmem_limit_bytes=limits["filter"] << 20),
    )(q, back, mid, last, xl, xr)
    return (filtered, advance)


def solution(mesh):
    placed = P(None, "gx", None, "gz")
    return jax.shard_map(
        shards,
        mesh=mesh,
        in_specs=(placed, placed),
        out_specs=(placed, placed),
        check_vma=False,
    )
```

```python
import functools
import math

import jax
import jax.numpy as jnp
import numpy as np
from jax import lax
from jax.experimental import pallas as pl
from jax.experimental.pallas import tpu as pltpu
from jax.sharding import PartitionSpec as P

alpha_deriv = 1.0 / 3.0
alpha_filter = 0.49
rows_edge = 32
rows_block = 64
rows_sub = 64
rows_local = 8
rows_smooth = 16
rows_carry = 16
limits = {"edges": 6, "local": 8, "advance": 10, "smooth": 6, "carry": 5, "filter": 8}
rows_filter = 32
near_deriv = 32
near_filter = 96
LANES = 128
bf16 = jnp.bfloat16
f32 = jnp.float32


def decay_rate(alpha):
    return (-1.0 + math.sqrt(1.0 - 4.0 * alpha * alpha)) / (2.0 * alpha)


def green_scale(alpha):
    return 1.0 / (1.0 + 2.0 * alpha * decay_rate(alpha))


def kernel_values(offsets, taps, alpha):
    offsets = np.asarray(offsets, dtype=np.float64)
    total = np.zeros_like(offsets)
    for shift, weight in taps.items():
        total = total + weight * green_scale(alpha) * np.power(
            decay_rate(alpha), np.abs(offsets - shift)
        )
    return total


def deriv_taps(spacing):
    near = 14.0 / 9.0 / (2.0 * spacing)
    far = 1.0 / 9.0 / (4.0 * spacing)
    return {1: near, -1: -near, 2: far, -2: -far}


def filter_taps():
    taps = {0: (11.0 + 10.0 * alpha_filter) / 16.0}
    weights = (
        (15.0 + 34.0 * alpha_filter) / 32.0,
        (-3.0 + 6.0 * alpha_filter) / 16.0,
        (1.0 - 2.0 * alpha_filter) / 32.0,
    )
    for shift, weight in enumerate(weights, 1):
        taps[shift] = 0.5 * weight
        taps[-shift] = 0.5 * weight
    return taps


def parts(values):
    high = values.astype(bf16)
    low = (values - high.astype(f32)).astype(bf16)
    return high, low


def np_parts(values):
    values = np.asarray(values, dtype=np.float32)
    high = values.astype(bf16)
    low = (values - high.astype(np.float32)).astype(bf16)
    return high, low


def band_matrix(count, taps, alpha, factor):
    source = np.arange(count)[:, None]
    target = np.arange(count)[None, :]
    high, low = np_parts(factor * kernel_values(source - target, taps, alpha))
    return np.concatenate([high, high, low], axis=0)


def edge_profiles(count, alpha, terms, group):
    cell = np.arange(count)
    table = np.zeros((2 * group, count))
    rate = decay_rate(alpha)
    for term in range(terms):
        if term < terms - 1:
            shape = (cell == term) * 1.0
        else:
            shape = np.where(cell >= term, np.power(rate, np.maximum(cell - term, 0)), 0.0)
        for comp in range(3):
            table[term * 3 + comp] = shape
            table[group + term * 3 + comp] = shape[::-1]
    return table


def padded_profiles(table):
    high, low = np_parts(table)
    rest = np.zeros((LANES - 3 * table.shape[0], table.shape[1]), dtype=bf16)
    return np.concatenate([high, high, low, rest], axis=0)


def component_masks(terms, group):
    lane = np.arange(LANES)
    row = lane % group
    masks = [(lane < 6 * group) & (row < 3 * terms) & (row % 3 == comp) for comp in range(3)]
    return jnp.asarray(np.stack(masks)[:, None, :], bf16)


def spread_columns(left, right):
    both = jnp.concatenate([left, right], axis=0)
    high = both.astype(bf16).astype(f32)
    low = both - high
    rest = jnp.zeros((128 - 3 * both.shape[0], both.shape[1]), f32)
    return jnp.concatenate([high, low, high, rest], axis=0).T.astype(bf16)


def dot(a, b):
    return jnp.dot(a, b, preferred_element_type=f32)


def rows_of(ref, chunk, size):
    return ref.at[:, pl.ds(chunk * size, size)]


def edge_body(
    rate, n_blocks,
    v_hbm, weight_ref, table_hbm,
    zright_ref, zleft_ref, xright_ref, xleft_ref, v_all, table_ref,
    sems,
):
    step = pl.program_id(0)
    cells, lines, count = v_all.shape[1:]
    size = cells // n_blocks

    def fetch(chunk):
        rows = pl.ds(chunk * size, size)
        return pltpu.make_async_copy(v_hbm.at[:, rows], v_all.at[:, rows], sems.at[chunk])

    table = pltpu.make_async_copy(table_hbm, table_ref, sems.at[n_blocks])

    @pl.when(step == 0)
    def _():
        for chunk in range(n_blocks):
            fetch(chunk).start()
        table.start()

    fetch(step).wait()
    v_ref = rows_of(v_all, step, size)
    near = weight_ref.shape[1]
    group = LANES // lines
    left_lane = lax.broadcasted_iota(jnp.int32, (LANES, LANES), 1) < LANES // 2
    for comp in range(3):
        for part in range(size // group):
            block = v_ref[comp, part * group:(part + 1) * group].reshape(LANES, count)
            both = jnp.where(left_lane, block[:, :LANES], block[:, count - LANES:]).T
            span = slice(part * LANES, (part + 1) * LANES)
            for term in range(2):
                row = term * 3 + comp
                zright_ref[row:row + 1, span] = jnp.sum(
                    both[LANES - near:] * weight_ref[term], axis=0, keepdims=True
                )
                zleft_ref[row:row + 1, span] = jnp.sum(
                    both[:near] * weight_ref[2 + term], axis=0, keepdims=True
                )
    for row in range(6, 8):
        zright_ref[row:row + 1, :] = jnp.zeros((1, size * lines), f32)
        zleft_ref[row:row + 1, :] = jnp.zeros((1, size * lines), f32)

    @pl.when(step == 0)
    def _():
        total = v_ref[:, near_deriv - 1]
        for i in range(near_deriv - 2, -1, -1):
            total = rate * total + v_ref[:, i]
        xleft_ref[0] = total
        xleft_ref[1] = v_ref[:, 0]

    @pl.when(step == pl.num_programs(0) - 1)
    def _():
        total = v_ref[:, size - near_deriv]
        for i in range(size - near_deriv + 1, size):
            total = rate * total + v_ref[:, i]
        xright_ref[0] = total
        xright_ref[1] = v_ref[:, size - 1]
        table.wait()


def weighted_rows(ref, weights):
    sums = [None] * 4
    for k, (row, weight) in enumerate(weights):
        term = weight * ref[:, row]
        sums[k % 4] = term if sums[k % 4] is None else sums[k % 4] + term
    return (sums[0] + sums[1]) + (sums[2] + sums[3])


def local_body(
    n_blocks, consts, v_all, prior_all, dz_ref, slope_all, back_all, base_all, heads_ref, tail
):
    step = pl.program_id(0)
    cells, lines, count = v_all.shape[1:]
    size = cells // n_blocks
    rate = consts["rate_d"]
    chunk = n_blocks - 1 - step
    v_ref, prior_ref, slope_ref, back_ref, base_ref = [
        rows_of(ref, chunk, size) for ref in (v_all, prior_all, slope_all, back_all, base_all)
    ]

    @pl.when(step == 0)
    def _():
        tail[...] = jnp.zeros_like(tail)

    sub = rows_local
    total = tail[...]
    for part in range(size // sub - 1, -1, -1):
        rows = slice(part * sub, (part + 1) * sub)
        hi, lo = parts(v_ref[:, rows].reshape(3 * sub * lines, count))
        lhs = jnp.concatenate([hi, lo, hi], axis=1)
        slope_ref[:, rows] = dot(lhs, dz_ref[...]).reshape(3, sub, lines, count)
        for i in range((part + 1) * sub - 1, part * sub - 1, -1):
            here = v_ref[:, i]
            total = here + rate * total
            back_ref[:, i] = total
            base_ref[:, i] = 2.4 * here - 0.68 * prior_ref[:, i]
    tail[...] = total
    heads_ref[chunk, 0] = total
    heads_ref[chunk, 1] = v_ref[:, 0]


def advance_body(
    n_blocks, consts,
    v_all, slope_all, back_all, base_all, heads_ref, xl_ref, xr_ref, zl_ref, zr_ref,
    pz_ref, mask_ref, weight_ref,
    adv_ref, prov_all, zright_ref, zleft_ref,
    extra, lead,
):
    step = pl.program_id(0)
    size, lines, count = adv_ref.shape[1:]
    v_ref, slope_ref, back_ref, base_ref, prov_ref = [
        rows_of(ref, step, size) for ref in (v_all, slope_all, back_all, base_all, prov_all)
    ]
    sub = rows_sub
    rate = consts["rate_d"]
    ratio = consts["ratio_d"]
    near = weight_ref.shape[1]

    @pl.when(step == 0)
    def _():
        before = (xl_ref[0] + rate * back_ref[:, 0]) * (1.0 / (1.0 - rate * rate))
        value = back_ref[:, 0] + rate * before
        lead[0] = value
        lead[1] = before + ratio * xl_ref[1]
        lead[2] = value + ratio * v_ref[:, 0]

    columns = spread_columns(zl_ref[...], zr_ref[...])
    edge = jnp.concatenate([columns * mask_ref[comp] for comp in range(3)], axis=0)
    extra[...] = dot(edge, pz_ref[...]).reshape(3, size, lines, count)
    last = step == n_blocks - 1
    following = jnp.minimum(step + 1, n_blocks - 1)
    beyond = jnp.where(last, xr_ref[0], 0.0)
    back_next = jnp.where(last, xr_ref[0], heads_ref[following, 0])
    here_next = jnp.where(last, xr_ref[1], heads_ref[following, 1])
    value, behind, level = lead[0], lead[1], lead[2]
    here = v_ref[:, 0]
    for part in range(size // sub):
        for i in range(part * sub, (part + 1) * sub):
            if i + 1 < size:
                ahead = v_ref[:, i + 1]
                back = back_ref[:, i + 1]
                if size - 1 - i <= near_deriv:
                    back = back + (rate ** (size - 1 - i)) * beyond
            else:
                ahead = here_next
                back = back_next
            value = back + rate * value
            above = value + ratio * ahead
            gx = above - behind
            behind = level
            level = above
            ux = consts["x_factor"] * here[0]
            adv = ux[None] * gx + here[2][None] * (slope_ref[:, i] + extra[:, i])
            adv_ref[:, i] = adv
            prov_ref[:, i] = base_ref[:, i] + adv
            here = ahead
        for comp in range(3):
            for piece in range(sub * lines // LANES):
                first = part * sub + piece * (LANES // lines)
                tile = prov_ref[comp, first:first + LANES // lines].reshape(LANES, count)
                lanes = slice(first * lines, first * lines + LANES)
                right = tile[:, count - LANES:].T
                left = tile[:, :LANES].T
                for ref, near_part, f0, f1, weight in (
                    (zright_ref, right[LANES - near:], right[127:128], right[126:127], weight_ref[0]),
                    (zleft_ref, left[:near], left[0:1], left[1:2], weight_ref[1]),
                ):
                    cs = consts["e3"] * jnp.sum(near_part * weight, axis=0, keepdims=True)
                    r = consts["rate_f"]
                    ref[comp:comp + 1, lanes] = r * cs + consts["e1"] * f0 + consts["e2"] * f1
                    ref[3 + comp:4 + comp, lanes] = (r * r) * cs + consts["e2"] * f0
                    ref[6 + comp:7 + comp, lanes] = (r * r * r) * cs
    lead[0] = value
    lead[1] = behind
    lead[2] = level
    for ref in (zright_ref, zleft_ref):
        ref[9:16, :] = jnp.zeros((7, size * lines), f32)


def smooth_body(n_blocks, consts, prov_all, fz_ref, q_all, xright_ref, xleft_ref, qsum):
    step = pl.program_id(0)
    cells, lines, count = prov_all.shape[1:]
    size = cells // n_blocks
    prov_ref, q_ref = [rows_of(ref, step, size) for ref in (prov_all, q_all)]
    rate = consts["rate_f"]

    @pl.when(step == 0)
    def _():
        qsum[...] = jnp.zeros_like(qsum)

    sub = rows_smooth
    for part in range(size // sub):
        rows = slice(part * sub, (part + 1) * sub)
        hi, lo = parts(prov_ref[:, rows].reshape(3 * sub * lines, count))
        lhs = jnp.concatenate([hi, lo, hi], axis=1)
        q_ref[:, rows] = dot(lhs, fz_ref[...]).reshape(3, sub, lines, count)
    for chunk_at in range((near_filter + size - 1) // size):
        offset = chunk_at * size
        used = min(size, near_filter - offset)

        @pl.when(step == chunk_at)
        def _():
            spots = [(i, rate ** (offset + i)) for i in range(used)]
            qsum[0] = qsum[0] + weighted_rows(q_ref, spots)

        @pl.when(step == n_blocks - 1 - chunk_at)
        def _():
            spots = [(size - 1 - i, rate ** (offset + i)) for i in range(used)]
            qsum[1] = qsum[1] + weighted_rows(q_ref, spots)

    @pl.when(step == 0)
    def _():
        xleft_ref[1] = q_ref[:, 0]
        xleft_ref[2] = q_ref[:, 1]

    @pl.when(step == n_blocks - 1)
    def _():
        xleft_ref[0] = qsum[0]
        xright_ref[0] = qsum[1]
        xright_ref[1] = q_ref[:, size - 1]
        xright_ref[2] = q_ref[:, size - 2]


def carry_body(n_blocks, rate, q_all, zl_ref, zr_ref, pz_ref, mask_ref, full_all, back_all, tail):
    step = pl.program_id(0)
    cells, lines, count = q_all.shape[1:]
    size = cells // n_blocks
    chunk = n_blocks - 1 - step
    q_ref, full_ref, back_ref = [rows_of(ref, chunk, size) for ref in (q_all, full_all, back_all)]

    @pl.when(step == 0)
    def _():
        tail[...] = jnp.zeros_like(tail)

    columns = spread_columns(zl_ref[...], zr_ref[...])
    masked = [columns * mask_ref[comp] for comp in range(3)]
    sub = rows_carry
    total = tail[...]
    for part in range(size // sub - 1, -1, -1):
        rows = slice(part * sub, (part + 1) * sub)
        flat = slice(part * sub * lines, (part + 1) * sub * lines)
        edge = jnp.concatenate([masked[comp][flat] for comp in range(3)], axis=0)
        full_ref[:, rows] = q_ref[:, rows] + dot(edge, pz_ref[...]).reshape(3, sub, lines, count)
        for i in range((part + 1) * sub - 1, part * sub - 1, -1):
            total = full_ref[:, i] + rate * total
            back_ref[:, i] = total
    tail[...] = total


def corner_body(xright_ref, xleft_ref, zl_ref, zr_ref, tr_ref, tl_ref, pz_ref, mask_ref, right_ref, left_ref):
    near = tr_ref.shape[0] // 3
    planes = jnp.concatenate([zl_ref[...], zr_ref[...]], axis=0)
    span = planes.shape[1]
    terms = right_ref.shape[0]
    lines = right_ref.shape[2]
    found = []
    for block, table in ((planes[:, span - near:], tr_ref), (planes[:, :near], tl_ref)):
        hi, lo = parts(block)
        found.append(dot(jnp.concatenate([hi, lo, hi], axis=1), table[...]))
    group = zl_ref.shape[0]
    both = jnp.concatenate(found, axis=1)
    columns = spread_columns(both[:group], both[group:])
    used = terms * lines
    columns = jnp.concatenate([columns[:used], columns[LANES:LANES + used]], axis=0)
    add = dot(jnp.concatenate([columns * mask_ref[comp] for comp in range(3)], axis=0), pz_ref[...])
    for comp in range(3):
        for term in range(terms):
            at = (2 * comp) * used + term * lines
            right_ref[term, comp] = xright_ref[term, comp] + add[at:at + lines]
            left_ref[term, comp] = xleft_ref[term, comp] + add[used + at:used + at + lines]


def filter_body(n_blocks, consts, q_all, back_all, xl_ref, xr_ref, out_ref, lead):
    step = pl.program_id(0)
    size = out_ref.shape[1]
    rate = consts["rate_f"]
    q_ref, back_ref = [rows_of(ref, step, size) for ref in (q_all, back_all)]
    last = step == n_blocks - 1
    following = rows_of(q_all, jnp.minimum(step + 1, n_blocks - 1), size)
    beyond = [jnp.where(last, xr_ref[1 + k], following[:, k]) for k in range(2)]

    @pl.when(step == 0)
    def _():
        lead[0] = (xl_ref[0] + rate * back_ref[:, 0]) * (1.0 / (1.0 - rate * rate))
        lead[1] = xl_ref[1]
        lead[2] = xl_ref[2]

    total, one, two = lead[0], lead[1], lead[2]
    here = q_ref[:, 0]
    ahead = q_ref[:, 1]
    for i in range(size):
        further = q_ref[:, i + 2] if i + 2 < size else beyond[i + 2 - size]
        total = back_ref[:, i] + rate * total
        out_ref[:, i] = (
            here
            + consts["s0"] * total
            + consts["s1"] * (ahead + one)
            + consts["s2"] * (further + two)
        )
        two = one
        one = here
        here = ahead
        ahead = further
    lead[0] = total
    lead[1] = one
    lead[2] = two
    for chunk_at in range((near_filter + size - 1) // size):
        offset = chunk_at * size

        @pl.when(step == n_blocks - 1 - chunk_at)
        def _():
            later = xr_ref[0]
            for k in range(min(size, near_filter - offset)):
                i = size - 1 - k
                weight = consts["s0"] * rate ** (offset + k + 1) / (1.0 - rate * rate)
                out_ref[:, i] = out_ref[:, i] + weight * later


def whole(shape):
    return pl.BlockSpec(shape, lambda t: (0,) * len(shape))


def in_hbm(values):
    return pltpu.with_memory_space_constraint(values, pltpu.HBM)


def ring(count, step):
    return [(i, (i + step) % count) for i in range(count)]


def swap(right, left, axis):
    count = lax.axis_size(axis)
    return (
        lax.ppermute(right, axis, ring(count, 1)),
        lax.ppermute(left, axis, ring(count, -1)),
    )


def shards(velocity, prior):
    comps, cells_x, lines, cells_z = velocity.shape
    spacing_x = 8.0 * math.pi / (cells_x * lax.axis_size("gx"))
    spacing_z = 3.0 * math.pi / (cells_z * lax.axis_size("gz"))
    dt_step = 0.3 / (1.0 / spacing_x + 1.0 / spacing_z)
    rate_d = decay_rate(alpha_deriv)
    rate_f = decay_rate(alpha_filter)
    size = rows_block
    n_blocks = cells_x // size
    span = cells_x * lines

    taps_x = deriv_taps(spacing_x)
    flat_part = taps_x[2] / alpha_deriv
    solve_part = (taps_x[1] - flat_part) * (-rate_d / alpha_deriv)
    kf = kernel_values([0, 1, 2, 3], filter_taps(), alpha_filter)
    half = filter_taps()
    t2 = half[3] / alpha_filter
    t1 = (half[2] - t2) / alpha_filter
    t0 = (half[1] - 3.0 * half[3] - t1) / alpha_filter
    rest = half[0] - 2.0 * half[2] - t0
    main = t0 + 2.0 * t2
    scale_f = 5.0 / 12.0 * main
    consts = {
        "rate_d": rate_d,
        "ratio_d": flat_part / solve_part,
        "x_factor": -dt_step * solve_part,
        "rate_f": rate_f,
        "s0": rest * (-rate_f / alpha_filter) / main,
        "s1": t1 / main,
        "s2": t2 / main,
        "e3": float(scale_f * kf[3] / rate_f**3),
        "e1": float(scale_f * (kf[1] - kf[3] / rate_f**2)),
        "e2": float(scale_f * (kf[2] - kf[3] / rate_f)),
    }

    plane = (comps, lines, cells_z)
    big = lambda rows, idx: pl.BlockSpec((comps, rows, lines, cells_z), lambda t: (0, idx(t), 0, 0))
    thin = lambda group, rows, idx: pl.BlockSpec((group, rows * lines), lambda t: (0, idx(t)))
    edge = (2,) + plane
    group_d = 8
    taps_z = deriv_taps(spacing_z)
    cell = np.arange(near_deriv)
    weights = np.stack(
        [-dt_step * kernel_values(cell - near_deriv - term, taps_z, alpha_deriv) for term in range(2)]
        + [-dt_step * kernel_values(cell + 1 + term, taps_z, alpha_deriv) for term in range(2)]
    )
    weights = jnp.asarray(np.broadcast_to(weights[:, :, None], (4, near_deriv, LANES)), f32)
    n_edge = cells_x // rows_edge
    held = pl.BlockSpec(memory_space=pltpu.VMEM)
    dz = jnp.asarray(band_matrix(cells_z, taps_z, alpha_deriv, -dt_step))
    zr_send, zl_send, xr_send, xl_send, field_in, dz = pl.pallas_call(
        functools.partial(edge_body, rate_d, n_edge),
        grid=(n_edge,),
        in_specs=[
            pl.BlockSpec(memory_space=pltpu.HBM), whole(weights.shape),
            pl.BlockSpec(memory_space=pltpu.HBM),
        ],
        out_specs=[thin(group_d, rows_edge, lambda t: t)] * 2 + [whole(edge)] * 2 + [held] * 2,
        out_shape=[jax.ShapeDtypeStruct((group_d, span), f32)] * 2
        + [jax.ShapeDtypeStruct(edge, f32)] * 2
        + [jax.ShapeDtypeStruct(velocity.shape, f32), jax.ShapeDtypeStruct(dz.shape, bf16)],
        scratch_shapes=[pltpu.SemaphoreType.DMA((n_edge + 1,))],
        name="edges",
        compiler_params=pltpu.CompilerParams(vmem_limit_bytes=limits["edges"] << 20),
    )(in_hbm(velocity), in_hbm(weights), in_hbm(dz))
    xl, xr = swap(xr_send, xl_send, "gx")
    zl, zr = swap(zr_send, zl_send, "gz")

    group_f = 16
    plain = lambda t: t
    edge3 = (3,) + plane
    block = (comps, size, lines, cells_z)
    field = jax.ShapeDtypeStruct(velocity.shape, f32)
    heads_shape = (n_blocks, 2) + plane
    slope, back, base, heads = pl.pallas_call(
        functools.partial(local_body, n_blocks, consts),
        grid=(n_blocks,),
        in_specs=[held, held, held],
        out_specs=[held, held, held, whole(heads_shape)],
        out_shape=[field] * 3 + [jax.ShapeDtypeStruct(heads_shape, f32)],
        scratch_shapes=[pltpu.VMEM(plane, f32)],
        name="local",
        compiler_params=pltpu.CompilerParams(vmem_limit_bytes=limits["local"] << 20),
        cost_estimate=pl.CostEstimate(flops=2 * 6144 * 768 * 256, bytes_accessed=25 << 20, transcendentals=0),
    )(field_in, prior, dz)

    pd = jnp.asarray(padded_profiles(edge_profiles(cells_z, alpha_deriv, 2, group_d)))
    mask_d = component_masks(2, group_d)
    decay = np.power(rate_f, np.arange(near_filter))
    decay = np.stack([decay[::-1], decay])
    decay = jnp.asarray(np.broadcast_to(decay[:, :, None], (2, near_filter, LANES)), f32)
    advance, prov, zr_send, zl_send = pl.pallas_call(
        functools.partial(advance_body, n_blocks, consts),
        grid=(n_blocks,),
        in_specs=[held, held, held, held] + [
            whole(heads_shape), whole(edge), whole(edge),
            thin(group_d, size, plain), thin(group_d, size, plain),
            whole(pd.shape), whole(mask_d.shape), whole(decay.shape),
        ],
        out_specs=[big(size, plain), held] + [thin(group_f, size, plain)] * 2,
        out_shape=[field] * 2 + [jax.ShapeDtypeStruct((group_f, span), f32)] * 2,
        scratch_shapes=[pltpu.VMEM(block, f32), pltpu.VMEM((3,) + plane, f32)],
        name="advance",
        compiler_params=pltpu.CompilerParams(vmem_limit_bytes=limits["advance"] << 20),
    )(field_in, slope, back, base, heads, xl, xr, zl, zr, pd, mask_d, decay)
    zl, zr = swap(zr_send, zl_send, "gz")

    fz = jnp.asarray(band_matrix(cells_z, filter_taps(), alpha_filter, scale_f))
    pf = jnp.asarray(padded_profiles(edge_profiles(cells_z, alpha_filter, 3, group_f)))
    mask_f = component_masks(3, group_f)
    q, xr_part, xl_part = pl.pallas_call(
        functools.partial(smooth_body, n_blocks, consts),
        grid=(n_blocks,),
        in_specs=[held, whole(fz.shape)],
        out_specs=[held, whole(edge3), whole(edge3)],
        out_shape=[field] + [jax.ShapeDtypeStruct(edge3, f32)] * 2,
        scratch_shapes=[pltpu.VMEM((2,) + plane, f32)],
        name="smooth",
        compiler_params=pltpu.CompilerParams(vmem_limit_bytes=limits["smooth"] << 20),
        cost_estimate=pl.CostEstimate(flops=2 * 6144 * 768 * 256, bytes_accessed=12 << 20, transcendentals=0),
    )(prov, fz)

    near = near_filter * lines
    cell = np.arange(cells_x)[:, None, None, None]
    line = (np.arange(lines)[None, :, None, None] == np.arange(lines)[None, None, None, :]) * 1.0
    grow = np.power(rate_f, cells_x - 1 - cell)
    pick = np.concatenate([grow, cell == cells_x - 1, cell == cells_x - 2], axis=2) * 1.0
    right_table = (pick * line).reshape(span, 3 * lines)
    left_table = (pick[::-1] * line).reshape(span, 3 * lines)
    widen = lambda t: np.concatenate([t, np.zeros((near, 128 - t.shape[1]))], axis=1)
    triple = lambda t: jnp.asarray(np.concatenate([np_parts(t)[k] for k in (0, 0, 1)], axis=0))
    tr = triple(widen(right_table[span - near:]))
    tl = triple(widen(left_table[:near]))
    xr_send, xl_send = pl.pallas_call(
        corner_body,
        grid=(1,),
        in_specs=[
            whole(edge3), whole(edge3), whole((group_f, span)), whole((group_f, span)),
            whole(tr.shape), whole(tl.shape), whole(pf.shape), whole(mask_f.shape),
        ],
        out_specs=[whole(edge3)] * 2,
        out_shape=[jax.ShapeDtypeStruct(edge3, f32)] * 2,
        name="corner",
        compiler_params=pltpu.CompilerParams(vmem_limit_bytes=8 << 20),
    )(xr_part, xl_part, zl, zr, tr, tl, pf, mask_f)
    xl, xr = swap(xr_send, xl_send, "gx")

    n_parts = cells_x // rows_filter
    backward = lambda t: n_parts - 1 - t
    q, back = pl.pallas_call(
        functools.partial(carry_body, n_parts, rate_f),
        grid=(n_parts,),
        in_specs=[
            held, thin(group_f, rows_filter, backward), thin(group_f, rows_filter, backward),
            whole(pf.shape), whole(mask_f.shape),
        ],
        out_specs=[held, held],
        out_shape=[field, field],
        scratch_shapes=[pltpu.VMEM(plane, f32)],
        name="carry",
        compiler_params=pltpu.CompilerParams(vmem_limit_bytes=limits["carry"] << 20),
        cost_estimate=pl.CostEstimate(flops=2 * 6144 * 128 * 256, bytes_accessed=12 << 20, transcendentals=0),
    )(q, zl, zr, pf, mask_f)
    filtered = pl.pallas_call(
        functools.partial(filter_body, n_parts, consts),
        grid=(n_parts,),
        in_specs=[held, held, whole(edge3), whole(edge3)],
        out_specs=big(rows_filter, plain),
        out_shape=field,
        scratch_shapes=[pltpu.VMEM((3,) + plane, f32)],
        name="filter",
        compiler_params=pltpu.CompilerParams(vmem_limit_bytes=limits["filter"] << 20),
    )(q, back, xl, xr)
    return (filtered, advance)


def solution(mesh):
    placed = P(None, "gx", None, "gz")
    return jax.shard_map(
        shards,
        mesh=mesh,
        in_specs=(placed, placed),
        out_specs=(placed, placed),
        check_vma=False,
    )
```
